256 devices in a mesh: section: 8 (over x, core), blk: 32 (over y, z).
Axes of the slice: x: 4, y: 4, z: 8, core: 2. Of those that a mesh axis runs over, the one named last changes fastest.
Arguments:
- hidden: bfloat16 [16384, 1536], P('blk'), may hold values from -6 to 6
- stale_kv: bfloat16 [8, 16384, 3072], P('section', 'blk'), may hold values from -6 to 6
- w_qkv: bfloat16 [8, 1536, 4608], P('section', 'blk'), may hold values from -0.15625 to 0.15625
- w_out: bfloat16 [8, 1536, 1536], P('section', 'blk'), may hold values from -0.15625 to 0.15625
- q_gain: float32 [8, 128], P('section'), may hold values from 0.25 to 1.75
- k_gain: float32 [8, 128], P('section'), may hold values from 0.25 to 1.75
- mod_table: float32 [8, 16, 3, 1536], P('section'), may hold values from -4 to 4
- pattern: int32 [128, 8], P('blk'), may hold values from 0 to 1, as said below
- step_index: int32 [128], P('blk'), may hold values from 0 to 15
- order: int32 [4], replicated, may hold values from 0 to 3, each once
Outputs:
- layer_out: bfloat16 [8, 16384, 1536], P('section', 'blk')
- kv_cache: bfloat16 [8, 16384, 3072], P('section', 'blk')
The draws below stay inside these ranges and needn't reach their ends.
Inputs may be any that keep to these rules, and one draw needn't show every extreme that they name: `pattern`: every row of the query tile's own tile (candidate c = tile index mod 4) is 1. `order`: names each patch once.
All inputs are finite; a program needn't handle non-finite values.
Results may differ from the reference program's by a relative error of at most 0.01.
Values may be sent and summed in bfloat16 or wider, within the bound.
A program may use at most 128 MiB of HBM per device.

```python
import math
import jax
import jax.numpy as jnp
from jax import lax

D = 1536
HEADS = 12
HDIM = 128
TILE = 128
PATCHES = 4
TSTEPS = 16
TOK_DEV = 128
INNER = 1536
SEQ_DEV = 512
SEQ = 16384
TPD = 4
QTILES = 128
N_SECTION = 8
N_BLK = 32


def draw_pattern(key, part):
    random_bits = jax.random.randint(key, (QTILES, 2 * TPD), 0, 2)
    own_tile = (jnp.arange(QTILES) % TPD)[:, None] == jnp.arange(2 * TPD)[None, :]
    return jnp.where(own_tile, 1, random_bits).astype(jnp.int32)


def set_ends(drawn, key, low, top_value):
    shape = drawn.shape
    place = [jax.random.randint(jax.random.fold_in(key, axis), (), 0, shape[axis]) for axis in range(len(shape))]
    drawn = drawn.at[tuple(place)].set(low)
    longest = shape.index(max(shape))
    place[longest] = (place[longest] + 1) % shape[longest]
    return drawn.at[tuple(place)].set(top_value)


def shard_levels(stream_key, dims, cuts, low, top_value):
    def one(dim, blocks):
        draws = jax.random.uniform(jax.random.fold_in(jax.random.fold_in(stream_key, 6), dim), (blocks,), jnp.float32, low / len(cuts), top_value / len(cuts))
        return jnp.repeat(jnp.exp(draws), dims[dim] // blocks).reshape((-1,) + (1,) * (len(dims) - dim - 1))

    factor_of = one(*cuts[0])
    for cut in cuts[1:]:
        factor_of = factor_of * one(*cut)
    return factor_of


def centred(stream_key, dims, scale, most, pieces=(), dtype=jnp.bfloat16):
    result = scale * jax.random.normal(stream_key, dims, jnp.float32)
    if pieces:
        result = result * shard_levels(stream_key, dims, pieces, -0.22, 0.18)
    return jnp.clip(result, -most, most).astype(dtype)


def setup_inputs(seed: int = 0) -> dict:
    key_list = jax.random.split(jax.random.key(seed), 11)
    return {
        "hidden": centred(key_list[0], (SEQ, D), 1.0, 6.0, ((0, 32),)),
        "stale_kv": centred(key_list[1], (N_SECTION, SEQ, 2 * INNER), 1.0, 6.0, ((0, 8), (1, 32))),
        "w_qkv": centred(key_list[2], (N_SECTION, D, 3 * INNER), D ** -0.5, 0.15625, ((0, 8), (1, 32))),
        "w_out": centred(key_list[3], (N_SECTION, INNER, D), INNER ** -0.5, 0.15625, ((0, 8), (1, 32))),
        "q_gain": jnp.clip(1.0 + 0.15 * jax.random.normal(key_list[4], (N_SECTION, HDIM), jnp.float32), 0.25, 1.75),
        "k_gain": jnp.clip(1.0 + 0.15 * jax.random.normal(key_list[5], (N_SECTION, HDIM), jnp.float32), 0.25, 1.75),
        "mod_table": centred(key_list[6], (N_SECTION, TSTEPS, 3, D), 0.5, 4.0, ((0, 8),), jnp.float32),
        "pattern": draw_pattern(jax.random.fold_in(key_list[10], 71), 0),
        "step_index": set_ends(jax.random.randint(key_list[8], (QTILES,), 0, TSTEPS), jax.random.fold_in(key_list[8], 1), 0, TSTEPS - 1).astype(jnp.int32),
        "order": jax.random.permutation(key_list[9], PATCHES).astype(jnp.int32),
    }


NORM_EPS = 1e-06

def layer_norm(values):
    centre = values - lax.optimization_barrier(jnp.mean(values, axis=-1, keepdims=True))
    spread = lax.optimization_barrier(jnp.mean(centre * centre, axis=-1, keepdims=True))
    return centre * lax.rsqrt(spread + NORM_EPS)

def head_norm(values, gain_row):
    square = lax.optimization_barrier(jnp.mean(values * values, axis=-1, keepdims=True))
    return values * lax.rsqrt(square + NORM_EPS) * gain_row

def reference(hidden, stale_kv, w_qkv, w_out, q_gain, k_gain, mod_table, pattern, step_index, order):
    inner_width = HEADS * HDIM
    tiles_patch = TOK_DEV // TILE
    shards = N_BLK
    current = hidden.reshape(shards, PATCHES, TOK_DEV, D)
    tile_steps_all = step_index.reshape(shards, PATCHES, tiles_patch)
    tile_mask_all = pattern.reshape(shards, PATCHES, tiles_patch, 2 * TPD)
    layer_list = []
    cache_list = []
    for layer in range(N_SECTION):
        kv_store = stale_kv[layer].reshape(shards, PATCHES, TOK_DEV, 2 * inner_width)
        modulation_table = mod_table[layer]
        results = jnp.zeros((shards, PATCHES, TOK_DEV, D), jnp.bfloat16)
        for slot in range(PATCHES):
            patch_id = order[slot].astype(jnp.int32)
            tokens = lax.dynamic_index_in_dim(current, patch_id, 1, keepdims=False)
            tile_steps = lax.dynamic_index_in_dim(tile_steps_all, patch_id, 1, keepdims=False)
            modulation = jnp.repeat(modulation_table[tile_steps], TILE, axis=1)
            shift_term = modulation[:, :, 0]
            scale_term = modulation[:, :, 1]
            gate_term = modulation[:, :, 2]
            modulated = (layer_norm(tokens.astype(jnp.float32)) * (1.0 + scale_term) + shift_term).astype(jnp.bfloat16)
            qkv = jnp.einsum('btd,de->bte', modulated.astype(jnp.float32), w_qkv[layer].astype(jnp.float32))
            fresh_kv = qkv[:, :, inner_width:].astype(jnp.bfloat16)
            kv_store = lax.dynamic_update_index_in_dim(kv_store, fresh_kv, patch_id, 1)
            queries = head_norm(qkv[:, :, :inner_width].reshape(shards, TOK_DEV, HEADS, HDIM), q_gain[layer]).astype(jnp.bfloat16)
            own_rows = kv_store.reshape(shards, SEQ_DEV, 2 * inner_width)
            previous = jnp.roll(own_rows, 1, axis=0)
            candidates = jnp.concatenate([own_rows, previous], axis=1)
            key_rows = head_norm(candidates[:, :, :inner_width].astype(jnp.float32).reshape(shards, 2 * SEQ_DEV, HEADS, HDIM), k_gain[layer]).astype(jnp.bfloat16)
            value_rows = candidates[:, :, inner_width:].reshape(shards, 2 * SEQ_DEV, HEADS, HDIM)
            scores = jnp.einsum('bqhd,bkhd->bhqk', queries.astype(jnp.float32), key_rows.astype(jnp.float32)) / math.sqrt(HDIM)
            tile_mask = lax.dynamic_index_in_dim(tile_mask_all, patch_id, 1, keepdims=False)
            token_mask = jnp.repeat(jnp.repeat(tile_mask, TILE, axis=1), TILE, axis=2).astype(jnp.float32)
            expo = jnp.exp(scores) * token_mask[:, None]
            weight_sum = lax.optimization_barrier(jnp.sum(expo, axis=-1))
            probs = expo.astype(jnp.bfloat16)
            mixture = jnp.einsum('bhqk,bkhd->bqhd', probs.astype(jnp.float32), value_rows.astype(jnp.float32))
            attended = (mixture / jnp.transpose(weight_sum, (0, 2, 1))[..., None]).reshape(shards, TOK_DEV, inner_width).astype(jnp.bfloat16)
            projected = jnp.einsum('bti,id->btd', attended.astype(jnp.float32), w_out[layer].astype(jnp.float32))
            output_rows = (tokens.astype(jnp.float32) + gate_term * projected).astype(jnp.bfloat16)
            results = lax.dynamic_update_index_in_dim(results, output_rows, patch_id, 1)
        layer_list.append(results.reshape(SEQ, D))
        cache_list.append(kv_store.reshape(SEQ, 2 * inner_width))
        current = results
    return (jnp.stack(layer_list), jnp.stack(cache_list))
```

```python
import math

import jax
import jax.numpy as jnp
from jax import lax
from jax.experimental import pallas as pl
from jax.experimental.pallas import tpu as pltpu
from jax.sharding import PartitionSpec as P

MESH = pl.DeviceIdType.MESH

D = 1536
HEADS = 12
HDIM = 128
PATCHES = 4
TSTEPS = 16
ROWS = 128
SEQ_DEV = PATCHES * ROWS
INNER = HEADS * HDIM
NY, NZ = 4, 8
NBLK = NY * NZ
NSEC = 8
SHARD = D // NBLK
NORM_EPS = 1e-06
CHUNK = 512
N_SEND = 70
SCORE_SCALE = math.log2(math.e) / math.sqrt(HDIM)


def head_norm(values, gain_row):
    square = jnp.mean(values * values, axis=-1, keepdims=True)
    return values * lax.rsqrt(square + NORM_EPS) * gain_row


def modulate(rows, scale, shift):
    values = rows.astype(jnp.float32)
    centre = values - jnp.mean(values, axis=-1, keepdims=True)
    spread = jnp.mean(centre * centre, axis=-1, keepdims=True)
    return (centre * lax.rsqrt(spread + NORM_EPS) * (1.0 + scale) + shift).astype(jnp.bfloat16)


def kernel(
    order_s, step_s, pattern_s, hidden_h, stale_h, wq_h, wo_h, qgain, kgain, mod_table,
    out_h, kv_h,
    wq, wo, keys, values, x_own, x_near, mod_own, mod_near, stale, hidden, fresh, out_rows, modulated, queries, attended,
    recv_q, recv_o, send, local, rx_own, rx_near, tx_own, tx_near, store_sem, rx_stale, tx_stale, rx_mod, tx_mod,
):
    sec = lax.axis_index("section")
    blk = lax.axis_index("blk")
    y, z = blk // NZ, lax.rem(blk, NZ)

    def at(yy, zz):
        return lax.rem(yy + 2 * NY, NY) * NZ + lax.rem(zz + 2 * NZ, NZ)

    up, down = lax.rem(sec + 1, NSEC), lax.rem(sec + NSEC - 1, NSEC)
    after, before = lax.rem(blk + 1, NBLK), lax.rem(blk + NBLK - 1, NBLK)
    zp, zm, yp, ym = at(y, z + 1), at(y, z - 1), at(y + 1, z), at(y - 1, z)

    load_hidden = pltpu.make_async_copy(hidden_h, hidden, local.at[0])
    load_stale = pltpu.make_async_copy(stale_h, stale, local.at[1])
    load_wq = pltpu.make_async_copy(wq_h, wq.at[pl.ds(blk * SHARD, SHARD)], local.at[2])
    load_wo = pltpu.make_async_copy(wo_h, wo.at[pl.ds(blk * SHARD, SHARD)], local.at[3])
    load_stale.start()
    load_hidden.start()
    load_wq.start()
    load_wo.start()

    barrier = pltpu.get_barrier_semaphore()
    for target in (
        (sec, zp), (sec, zm), (sec, yp), (sec, ym), (sec, after), (sec, before),
        (up, blk), (down, blk), (up, after), (down, before),
    ):
        pl.semaphore_signal(barrier, inc=1, device_id=target, device_id_type=MESH)
    pl.semaphore_wait(barrier, 10)

    sends = []

    def push(which, shard, target, source=None):
        buffer, recv = (wq, recv_q) if which == "q" else (wo, recv_o)
        rows = buffer.at[pl.ds(shard * SHARD, SHARD)]
        copy = pltpu.make_async_remote_copy(
            src_ref=rows if source is None else source,
            dst_ref=rows,
            send_sem=send.at[len(sends)],
            recv_sem=recv.at[shard],
            device_id=(sec, target),
            device_id_type=MESH,
        )
        copy.start()
        sends.append(copy)

    def arrived(which, shard):
        buffer, recv = (wq, recv_q) if which == "q" else (wo, recv_o)
        rows = buffer.at[pl.ds(shard * SHARD, SHARD)]
        pltpu.make_async_remote_copy(
            src_ref=rows, dst_ref=rows, send_sem=send.at[0], recv_sem=recv.at[shard],
            device_id=(sec, blk), device_id_type=MESH,
        ).wait_recv()

    push("o", blk, yp, wo_h)
    push("o", blk, ym, wo_h)
    push("q", blk, zp, wq_h)
    push("q", blk, zm, wq_h)
    push("q", blk, yp, wq_h)
    push("q", blk, ym, wq_h)
    push("o", blk, zp, wo_h)
    push("o", blk, zm, wo_h)

    for slot in range(PATCHES):
        step = step_s[order_s[slot]]
        for row in range(3):
            mod_own[slot, pl.ds(row, 1), :] = mod_table[pl.ds(3 * step + row, 1), :]
    send_mod = pltpu.make_async_remote_copy(
        src_ref=mod_own, dst_ref=mod_near, send_sem=tx_mod, recv_sem=rx_mod,
        device_id=(sec, after), device_id_type=MESH,
    )
    send_mod.start()

    load_hidden.wait()

    def near_copy(slot):
        return pltpu.make_async_remote_copy(
            src_ref=x_own.at[slot], dst_ref=x_near.at[slot], send_sem=tx_near.at[slot], recv_sem=rx_near.at[slot],
            device_id=(sec, after), device_id_type=MESH,
        )

    @pl.when(sec == 0)
    def _():
        for slot in range(PATCHES):
            x_own[slot] = hidden[order_s[slot]]
        for slot in range(PATCHES):
            near_copy(slot).start()

    load_stale.wait()
    for slot in range(1, PATCHES):
        patch = order_s[slot]
        for head in range(HEADS):
            columns = pl.ds(head * HDIM, HDIM)
            keys[pl.ds(slot * ROWS, ROWS), columns] = head_norm(
                stale[patch, :, columns].astype(jnp.float32), kgain[...]
            ).astype(jnp.bfloat16)
        values[pl.ds(slot * ROWS, ROWS), :] = stale[patch, :, INNER:]
    stale_sends = []
    for index, buffer in enumerate((keys, values)):
        copy = pltpu.make_async_remote_copy(
            src_ref=buffer.at[pl.ds(ROWS, SEQ_DEV - ROWS)],
            dst_ref=buffer.at[pl.ds(SEQ_DEV + ROWS, SEQ_DEV - ROWS)],
            send_sem=tx_stale.at[index], recv_sem=rx_stale.at[index],
            device_id=(sec, after), device_id_type=MESH,
        )
        copy.start()
        stale_sends.append(copy)

    even = lax.rem(z, 2) == 0
    arrived("o", ym)
    arrived("o", yp)
    push("o", jnp.where(even, ym, yp), jnp.where(even, yp, ym))
    for shard in (ym, yp):
        push("o", shard, zp)
        push("o", shard, zm)
    arrived("o", at(y + 2, z))
    push("o", at(y + 2, z), zp)
    push("o", at(y + 2, z), zm)

    def cross(zk):
        arrived("q", at(y - 1, zk))
        arrived("q", at(y + 1, zk))
        odd = lax.rem(zk + NZ, 2) == 1
        push("q", jnp.where(odd, at(y + 1, zk), at(y - 1, zk)), jnp.where(odd, ym, yp))

    previous = z
    for k in range(1, NZ):
        if k == NZ - 1:
            zk, forward = z + NZ // 2, None
        elif k % 2 == 1:
            zk, forward = z - (k + 1) // 2, (zp if k < NZ - 3 else None)
        else:
            zk, forward = z + k // 2, zm
        arrived("q", at(y, zk))
        if forward is not None:
            push("q", at(y, zk), forward)
        push("q", at(y, zk), yp)
        push("q", at(y, zk), ym)
        cross(previous)
        for i in range(NY):
            arrived("o", at(y + i, zk))
            if forward is not None:
                push("o", at(y + i, zk), forward)
        previous = zk
    cross(previous)
    for i in range(NZ):
        arrived("q", at(y + 2, z + i))
    load_wq.wait()
    load_wo.wait()
    send_mod.wait()
    for copy in stale_sends:
        copy.wait()

    def slot_step(slot, carry):
        @pl.when(sec > 0)
        def _():
            pltpu.make_async_remote_copy(
                src_ref=x_own.at[slot], dst_ref=x_own.at[slot], send_sem=tx_own.at[slot], recv_sem=rx_own.at[slot],
                device_id=(up, blk), device_id_type=MESH,
            ).wait_recv()

        modulated[pl.ds(0, ROWS), :] = modulate(
            x_own[slot], mod_own[slot, pl.ds(1, 1), :], mod_own[slot, pl.ds(0, 1), :]
        )
        near_copy(slot).wait_recv()
        modulated[pl.ds(ROWS, ROWS), :] = modulate(
            x_near[slot], mod_near[slot, pl.ds(1, 1), :], mod_near[slot, pl.ds(0, 1), :]
        )
        own_rows = pl.ds(pl.multiple_of(slot * ROWS, ROWS), ROWS)
        near_rows = pl.ds(pl.multiple_of(SEQ_DEV + slot * ROWS, ROWS), ROWS)

        def project_q(chunk, carry):
            base = pl.multiple_of(chunk * CHUNK, CHUNK)
            product = jnp.dot(
                modulated[pl.ds(0, ROWS), :], wq[:, pl.ds(base, CHUNK)], preferred_element_type=jnp.float32
            )
            for head in range(CHUNK // HDIM):
                queries[:, pl.ds(base + head * HDIM, HDIM)] = head_norm(
                    product[:, head * HDIM:(head + 1) * HDIM], qgain[...]
                ).astype(jnp.bfloat16)
            return carry

        def project_k(chunk, carry):
            base = pl.multiple_of(chunk * CHUNK, CHUNK)
            product = jnp.dot(
                modulated[...], wq[:, pl.ds(INNER + base, CHUNK)], preferred_element_type=jnp.float32
            ).astype(jnp.bfloat16)
            fresh[slot, :, pl.ds(base, CHUNK)] = product[:ROWS]
            for head in range(CHUNK // HDIM):
                normed = head_norm(
                    product[:, head * HDIM:(head + 1) * HDIM].astype(jnp.float32), kgain[...]
                ).astype(jnp.bfloat16)
                columns = pl.ds(base + head * HDIM, HDIM)
                keys[own_rows, columns] = normed[:ROWS]
                keys[near_rows, columns] = normed[ROWS:]
            return carry

        def project_v(chunk, carry):
            base = pl.multiple_of(chunk * CHUNK, CHUNK)
            product = jnp.dot(
                modulated[...], wq[:, pl.ds(2 * INNER + base, CHUNK)], preferred_element_type=jnp.float32
            ).astype(jnp.bfloat16)
            fresh[slot, :, pl.ds(INNER + base, CHUNK)] = product[:ROWS]
            values[own_rows, pl.ds(base, CHUNK)] = product[:ROWS]
            values[near_rows, pl.ds(base, CHUNK)] = product[ROWS:]
            return carry

        lax.fori_loop(0, INNER // CHUNK, project_q, 0)
        lax.fori_loop(0, INNER // CHUNK, project_k, 0)
        lax.fori_loop(0, INNER // CHUNK, project_v, 0)
        pltpu.make_async_copy(fresh.at[slot], kv_h.at[slot], store_sem.at[0, slot]).start()

        patch = order_s[slot]
        masks = [
            pattern_s[patch, half * PATCHES + order_s[j]].astype(jnp.float32) for half in range(2) for j in range(PATCHES)
        ]

        def attend(head, carry):
            columns = pl.ds(pl.multiple_of(head * HDIM, HDIM), HDIM)
            scores = lax.dot_general(
                queries[:, columns], keys[:, columns], (((1,), (1,)), ((), ())), preferred_element_type=jnp.float32
            )
            tiles = [
                jnp.exp2(scores[:, j * ROWS:(j + 1) * ROWS] * SCORE_SCALE) * masks[j] for j in range(2 * PATCHES)
            ]
            total = tiles[0]
            for tile in tiles[1:]:
                total = total + tile
            weight_sum = jnp.sum(total, axis=-1, keepdims=True)
            probs = jnp.concatenate([tile.astype(jnp.bfloat16) for tile in tiles], axis=1)
            mixture = jnp.dot(probs, values[:, columns], preferred_element_type=jnp.float32)
            attended[:, columns] = (mixture / weight_sum).astype(jnp.bfloat16)
            return carry

        lax.fori_loop(0, HEADS, attend, 0, unroll=2)

        def project_out(chunk, carry):
            columns = pl.ds(pl.multiple_of(chunk * CHUNK, CHUNK), CHUNK)
            product = jnp.dot(attended[...], wo[:, columns], preferred_element_type=jnp.float32)
            out_rows[slot, :, columns] = (
                x_own[slot, :, columns].astype(jnp.float32) + mod_own[slot, pl.ds(2, 1), columns] * product
            ).astype(jnp.bfloat16)
            return carry

        lax.fori_loop(0, D // CHUNK, project_out, 0)

        @pl.when(sec < NSEC - 1)
        def _():
            for target, landing, tx, rx in ((blk, x_own, tx_own, rx_own), (after, x_near, tx_near, rx_near)):
                pltpu.make_async_remote_copy(
                    src_ref=out_rows.at[slot], dst_ref=landing.at[slot], send_sem=tx.at[slot], recv_sem=rx.at[slot],
                    device_id=(up, target), device_id_type=MESH,
                ).start()

        pltpu.make_async_copy(out_rows.at[slot], out_h.at[slot], store_sem.at[1, slot]).start()
        return carry

    @pl.when(sec == 0)
    def _():
        for slot in range(PATCHES):
            near_copy(slot).wait_send()

    lax.fori_loop(0, PATCHES, slot_step, 0)

    for copy in sends:
        copy.wait_send()
    for slot in range(PATCHES):
        pltpu.make_async_copy(fresh.at[slot], kv_h.at[slot], store_sem.at[0, slot]).wait()
        pltpu.make_async_copy(out_rows.at[slot], out_h.at[slot], store_sem.at[1, slot]).wait()

    @pl.when(sec < NSEC - 1)
    def _():
        for slot in range(PATCHES):
            for tx in (tx_own, tx_near):
                pltpu.make_async_remote_copy(
                    src_ref=out_rows.at[slot], dst_ref=x_own.at[slot], send_sem=tx.at[slot], recv_sem=rx_own.at[slot],
                    device_id=(up, blk), device_id_type=MESH,
                ).wait_send()


def to_patch_order(order_s, rows_in, kv_in, rows_out, kv_out):
    rows_out[...] = rows_in[...]
    kv_out[...] = kv_in[...]


def on_device(hidden, stale_kv, w_qkv, w_out, q_gain, k_gain, mod_table, pattern, step_index, order):
    vmem, smem, anywhere = (
        pl.BlockSpec(memory_space=pltpu.VMEM),
        pl.BlockSpec(memory_space=pltpu.SMEM),
        pl.BlockSpec(memory_space=pl.ANY),
    )
    bf16, f32 = jnp.bfloat16, jnp.float32
    dma = pltpu.SemaphoreType.DMA
    rows_slots, kv_slots = pl.pallas_call(
        kernel,
        out_shape=(
            jax.ShapeDtypeStruct((PATCHES, ROWS, D), bf16),
            jax.ShapeDtypeStruct((PATCHES, ROWS, 2 * INNER), bf16),
        ),
        in_specs=[smem] * 3 + [anywhere] * 4 + [vmem] * 3,
        out_specs=(anywhere, anywhere),
        scratch_shapes=[
            pltpu.VMEM((D, 3 * INNER), bf16),
            pltpu.VMEM((INNER, D), bf16),
            pltpu.VMEM((2 * SEQ_DEV, INNER), bf16),
            pltpu.VMEM((2 * SEQ_DEV, INNER), bf16),
            pltpu.VMEM((PATCHES, ROWS, D), bf16),
            pltpu.VMEM((PATCHES, ROWS, D), bf16),
            pltpu.VMEM((PATCHES, 8, D), f32),
            pltpu.VMEM((PATCHES, 8, D), f32),
            pltpu.VMEM((PATCHES, ROWS, 2 * INNER), bf16),
            pltpu.VMEM((PATCHES, ROWS, D), bf16),
            pltpu.VMEM((PATCHES, ROWS, 2 * INNER), bf16),
            pltpu.VMEM((PATCHES, ROWS, D), bf16),
            pltpu.VMEM((2 * ROWS, D), bf16),
            pltpu.VMEM((ROWS, INNER), bf16),
            pltpu.VMEM((ROWS, INNER), bf16),
            dma((NBLK,)),
            dma((NBLK,)),
            dma((N_SEND,)),
            dma((4,)),
            dma((PATCHES,)),
            dma((PATCHES,)),
            dma((PATCHES,)),
            dma((PATCHES,)),
            dma((2, PATCHES)),
            dma((2,)),
            dma((2,)),
            dma(()),
            dma(()),
        ],
        compiler_params=pltpu.CompilerParams(
            collective_id=0, has_side_effects=True, vmem_limit_bytes=63 * 1024 * 1024
        ),
        name="pipeline",
    )(
        order, step_index, pattern,
        hidden.reshape(PATCHES, ROWS, D), stale_kv.reshape(PATCHES, ROWS, 2 * INNER), w_qkv[0], w_out[0],
        q_gain, k_gain, mod_table.reshape(TSTEPS * 3, D),
    )

    def slot_of(patch, order_ref):
        slot = jnp.int32(0)
        for index in range(1, PATCHES):
            slot = jnp.where(order_ref[index] == patch, index, slot)
        return (slot, 0, 0)

    layer_out, kv_cache = pl.pallas_call(
        to_patch_order,
        out_shape=(
            jax.ShapeDtypeStruct((PATCHES, ROWS, D), bf16),
            jax.ShapeDtypeStruct((PATCHES, ROWS, 2 * INNER), bf16),
        ),
        grid_spec=pltpu.PrefetchScalarGridSpec(
            num_scalar_prefetch=1,
            grid=(PATCHES,),
            in_specs=[pl.BlockSpec((1, ROWS, D), slot_of), pl.BlockSpec((1, ROWS, 2 * INNER), slot_of)],
            out_specs=[
                pl.BlockSpec((1, ROWS, D), lambda patch, order_ref: (patch, 0, 0)),
                pl.BlockSpec((1, ROWS, 2 * INNER), lambda patch, order_ref: (patch, 0, 0)),
            ],
        ),
        name="patch_order",
    )(order, rows_slots, kv_slots)
    return (layer_out.reshape(1, SEQ_DEV, D), kv_cache.reshape(1, SEQ_DEV, 2 * INNER))


def solution(mesh):
    in_specs = (
        P("blk", None),
        P("section", "blk", None),
        P("section", "blk", None),
        P("section", "blk", None),
        P("section", None),
        P("section", None),
        P("section", None, None, None),
        P("blk", None),
        P("blk"),
        P(),
    )
    out_specs = (P("section", "blk", None), P("section", "blk", None))
    return jax.shard_map(
        on_device, mesh=mesh, in_specs=in_specs, out_specs=out_specs, check_vma=False
    )
```

```python
import math

import jax
import jax.numpy as jnp
from jax import lax
from jax.experimental import pallas as pl
from jax.experimental.pallas import tpu as pltpu
from jax.sharding import PartitionSpec as P

MESH = pl.DeviceIdType.MESH

D = 1536
HEADS = 12
HDIM = 128
PATCHES = 4
TSTEPS = 16
ROWS = 128
SEQ_DEV = PATCHES * ROWS
INNER = HEADS * HDIM
NY, NZ = 4, 8
NBLK = NY * NZ
NSEC = 8
SHARD = D // NBLK
NORM_EPS = 1e-06
CHUNK = 768
SPLIT_QKV, SPLIT_OUT = 2560, 1024
OFFSETS = (0, 1, -1, 2, -2, 3, 4, 5)
FAR_UP, FAR_DOWN = 5, 2
HELPED = 2
HELPERS = NSEC - HELPED
SCORE_SCALE = math.log2(math.e) / math.sqrt(HDIM)


def head_norm(values, gain_row):
    square = jnp.mean(values * values, axis=-1, keepdims=True)
    return values * lax.rsqrt(square + NORM_EPS) * gain_row


def modulate(rows, scale, shift):
    values = rows.astype(jnp.float32)
    centre = values - jnp.mean(values, axis=-1, keepdims=True)
    spread = jnp.mean(centre * centre, axis=-1, keepdims=True)
    return (centre * lax.rsqrt(spread + NORM_EPS) * (1.0 + scale) + shift).astype(jnp.bfloat16)


def kernel(
    order_s, step_s, pattern_s, hidden_h, stale_h, wq_h, wo_h, qgain, kgain, mod_table,
    out_h, kv_h,
    wq, wo, wo_help, keys, values, x_own, x_near, mod_own, mod_near, stale, hidden, fresh, out_rows, modulated, queries, attended,
    recv_a, recv_b, recv_o, recv_p, recv_h, send_a, send_b, send_o, send_p, send_h, send_x, local, rx_own, rx_near, tx_own, tx_near, store_sem, rx_stale, tx_stale, rx_mod, tx_mod,
):
    sec = lax.axis_index("section")
    blk = lax.axis_index("blk")
    y, z = blk // NZ, lax.rem(blk, NZ)

    def at(yy, zz):
        return lax.rem(yy + 2 * NY, NY) * NZ + lax.rem(zz + 2 * NZ, NZ)

    up, down = lax.rem(sec + 1, NSEC), lax.rem(sec + NSEC - 1, NSEC)
    after, before = lax.rem(blk + 1, NBLK), lax.rem(blk + NBLK - 1, NBLK)
    chip_up, chip_down = lax.rem(sec + 2, NSEC), lax.rem(sec + NSEC - 2, NSEC)
    zp, zm, yp, ym = at(y, z + 1), at(y, z - 1), at(y + 1, z), at(y - 1, z)

    load_hidden = pltpu.make_async_copy(hidden_h, hidden, local.at[0])
    load_stale = pltpu.make_async_copy(stale_h, stale, local.at[1])
    load_wq = pltpu.make_async_copy(wq_h, wq.at[pl.ds(blk * SHARD, SHARD)], local.at[2])
    load_wo = pltpu.make_async_copy(wo_h, wo.at[pl.ds(blk * SHARD, SHARD)], local.at[3])
    load_stale.start()
    load_hidden.start()
    load_wq.start()
    load_wo.start()

    barrier = pltpu.get_barrier_semaphore()
    for target in (
        (sec, zp), (sec, zm), (sec, yp), (sec, ym), (sec, after), (sec, before),
        (up, blk), (down, blk), (up, after), (down, before), (chip_up, blk), (chip_down, blk),
    ):
        pl.semaphore_signal(barrier, inc=1, device_id=target, device_id_type=MESH)
    pl.semaphore_wait(barrier, 12)


    class Gather:
        def __init__(self, buffer, start, stop, recv, send, source):
            self.buffer, self.columns = buffer, pl.ds(start, stop - start)
            self.recv, self.send, self.source = recv, send, source
            self.count = 0

        def rows(self, shard):
            return self.buffer.at[pl.ds(pl.multiple_of(shard * SHARD, 16), SHARD), self.columns]

        def push(self, shard, *targets, from_input=False, to=None):
            for target in targets:
                copy = pltpu.make_async_remote_copy(
                    src_ref=self.source.at[:, self.columns] if from_input else self.rows(shard),
                    dst_ref=(self if to is None else to).rows(shard),
                    send_sem=self.send.at[self.count],
                    recv_sem=(self if to is None else to).recv.at[shard],
                    device_id=target if isinstance(target, tuple) else (sec, target),
                    device_id_type=MESH,
                )
                copy.start()
                self.count += 1

        def arrived(self, shard):
            pltpu.make_async_remote_copy(
                src_ref=self.rows(shard), dst_ref=self.rows(shard), send_sem=self.send.at[0],
                recv_sem=self.recv.at[shard], device_id=(up, blk), device_id_type=MESH,
            ).wait_recv()

        def along(self, shard, k):
            if OFFSETS[k] == 0:
                self.push(shard, zp, zm)
            elif 0 < OFFSETS[k] < FAR_UP:
                self.push(shard, zm)
            elif -FAR_DOWN < OFFSETS[k] < 0:
                self.push(shard, zp)

        def cross(self, k, level):
            zk = z + OFFSETS[k]
            here, there = at(y - 1, zk), at(y + 1, zk)
            self.arrived(here)
            self.arrived(there)
            if level:
                odd = lax.rem(zk + 2 * NZ, 2) == 1
                self.push(jnp.where(odd, there, here), jnp.where(odd, ym, yp))
            else:
                self.push(there, ym)
            return here, there

        def wait_sends(self):
            for index in range(self.count):
                pltpu.make_async_remote_copy(
                    src_ref=self.rows(blk), dst_ref=self.rows(blk), send_sem=self.send.at[index],
                    recv_sem=self.recv.at[blk], device_id=(up, blk), device_id_type=MESH,
                ).wait_send()

    def gather(main, side, level, extras=()):
        side.arrived(ym)
        side.arrived(yp)
        if level:
            even = lax.rem(z, 2) == 0
            side.push(jnp.where(even, ym, yp), jnp.where(even, yp, ym))
        else:
            side.push(yp, ym)
        side.push(ym, zp, zm)
        side.push(yp, zp, zm)
        for k in range(1, NZ):
            shard = at(y, z + OFFSETS[k])
            main.arrived(shard)
            main.along(shard, k)
            main.push(shard, yp, ym)
            if k == 1:
                side.arrived(at(y + 2, z))
                side.push(at(y + 2, z), zp, zm)
            main.cross(k - 1, level)
            for i in range(NY):
                shard = at(y + i, z + OFFSETS[k])
                side.arrived(shard)
                side.along(shard, k)
            if k - 1 < len(extras):
                extras[k - 1].start()
        main.cross(NZ - 1, level)
        for k in range(NZ):
            main.arrived(at(y + 2, z + OFFSETS[k]))

    qkv_main = Gather(wq, 0, SPLIT_QKV, recv_a, send_a, wq_h)
    qkv_side = Gather(wq, SPLIT_QKV, 3 * INNER, recv_b, send_b, wq_h)
    out_main = Gather(wo, 0, SPLIT_OUT, recv_o, send_o, wo_h)
    out_side = Gather(wo, SPLIT_OUT, D, recv_p, send_p, wo_h)
    help_out = Gather(wo_help, 0, D, recv_h, send_h, wo_h)
    helped_out = Gather(wo, 0, D, recv_o, send_x, wo_h)

    @pl.when(sec < HELPED)
    def _():
        helped_out.push(blk, (chip_down, blk), from_input=True, to=help_out)

    @pl.when(sec >= HELPERS)
    def _():
        for k in range(NZ):
            shard = at(y, z + OFFSETS[k])
            help_out.arrived(shard)
            help_out.along(shard, k)
            help_out.push(shard, yp, ym)
            if k > 0:
                help_out.push(shard, (chip_up, blk), to=helped_out)
                for shard in help_out.cross(k - 1, True):
                    help_out.push(shard, (chip_up, blk), to=helped_out)
            if k > 1:
                shard = at(y + 2, z + OFFSETS[k - 2])
                help_out.arrived(shard)
                help_out.push(shard, (chip_up, blk), to=helped_out)
        for shard in help_out.cross(NZ - 1, True):
            help_out.push(shard, (chip_up, blk), to=helped_out)
        for k in (NZ - 2, NZ - 1):
            shard = at(y + 2, z + OFFSETS[k])
            help_out.arrived(shard)
            help_out.push(shard, (chip_up, blk), to=helped_out)

    qkv_side.push(blk, yp, ym, from_input=True)
    qkv_main.push(blk, zp, zm, yp, ym, from_input=True)
    qkv_side.push(blk, zp, zm, from_input=True)

    for slot in range(PATCHES):
        step = step_s[order_s[slot]]
        for row in range(3):
            mod_own[pl.ds(4 * slot + row, 1), :] = mod_table[pl.ds(3 * step + row, 1), :]
    send_mod = pltpu.make_async_remote_copy(
        src_ref=mod_own, dst_ref=mod_near, send_sem=tx_mod, recv_sem=rx_mod,
        device_id=(sec, after), device_id_type=MESH,
    )
    send_mod.start()

    load_hidden.wait()

    def near_copy(slot):
        return pltpu.make_async_remote_copy(
            src_ref=x_own.at[slot], dst_ref=x_near.at[slot], send_sem=tx_near.at[slot], recv_sem=rx_near.at[slot],
            device_id=(sec, after), device_id_type=MESH,
        )

    @pl.when(sec == 0)
    def _():
        for slot in range(PATCHES):
            x_own[slot] = hidden[order_s[slot]]
        near_copy(0).start()

    load_stale.wait()
    for slot in range(1, PATCHES):
        patch = order_s[slot]
        for head in range(HEADS):
            columns = pl.ds(head * HDIM, HDIM)
            keys[pl.ds(slot * ROWS, ROWS), columns] = head_norm(
                stale[patch, :, columns].astype(jnp.float32), kgain[...]
            ).astype(jnp.bfloat16)
        values[pl.ds(slot * ROWS, ROWS), :] = stale[patch, :, INNER:]
    stale_copies = []
    for slot in range(1, PATCHES):
        for index, buffer in enumerate((keys, values)):
            stale_copies.append(pltpu.make_async_remote_copy(
                src_ref=buffer.at[pl.ds(slot * ROWS, ROWS)],
                dst_ref=buffer.at[pl.ds(SEQ_DEV + slot * ROWS, ROWS)],
                send_sem=tx_stale.at[index, slot], recv_sem=rx_stale.at[index, slot],
                device_id=(sec, after), device_id_type=MESH,
            ))

    gather(qkv_main, qkv_side, False, stale_copies)

    @pl.when(sec == 0)
    def _():
        for slot in range(1, PATCHES):
            near_copy(slot).start()

    @pl.when(sec >= HELPED)
    def _():
        out_side.push(blk, yp, ym, from_input=True)
        out_main.push(blk, zp, zm, yp, ym, from_input=True)
        out_side.push(blk, zp, zm, from_input=True)
        gather(out_main, out_side, True)

    load_wq.wait()
    load_wo.wait()
    send_mod.wait()
    for copy in stale_copies:
        copy.wait()

    def slot_step(slot, carry):
        @pl.when(sec > 0)
        def _():
            pltpu.make_async_remote_copy(
                src_ref=x_own.at[slot], dst_ref=x_own.at[slot], send_sem=tx_own.at[slot], recv_sem=rx_own.at[slot],
                device_id=(up, blk), device_id_type=MESH,
            ).wait_recv()

        modulated[pl.ds(0, ROWS), :] = modulate(
            x_own[slot], mod_own[pl.ds(4 * slot + 1, 1), :], mod_own[pl.ds(4 * slot, 1), :]
        )
        near_copy(slot).wait_recv()
        modulated[pl.ds(ROWS, ROWS), :] = modulate(
            x_near[slot], mod_near[pl.ds(4 * slot + 1, 1), :], mod_near[pl.ds(4 * slot, 1), :]
        )
        own_rows = pl.ds(pl.multiple_of(slot * ROWS, ROWS), ROWS)
        near_rows = pl.ds(pl.multiple_of(SEQ_DEV + slot * ROWS, ROWS), ROWS)

        def project_q(chunk, carry):
            base = pl.multiple_of(chunk * CHUNK, CHUNK)
            product = jnp.dot(
                modulated[pl.ds(0, ROWS), :], wq[:, pl.ds(base, CHUNK)], preferred_element_type=jnp.float32
            )
            for head in range(CHUNK // HDIM):
                queries[:, pl.ds(base + head * HDIM, HDIM)] = head_norm(
                    product[:, head * HDIM:(head + 1) * HDIM], qgain[...]
                ).astype(jnp.bfloat16)
            return carry

        def project_k(chunk, carry):
            base = pl.multiple_of(chunk * CHUNK, CHUNK)
            product = jnp.dot(
                modulated[...], wq[:, pl.ds(INNER + base, CHUNK)], preferred_element_type=jnp.float32
            ).astype(jnp.bfloat16)
            fresh[slot, :, pl.ds(base, CHUNK)] = product[:ROWS]
            for head in range(CHUNK // HDIM):
                normed = head_norm(
                    product[:, head * HDIM:(head + 1) * HDIM].astype(jnp.float32), kgain[...]
                ).astype(jnp.bfloat16)
                columns = pl.ds(base + head * HDIM, HDIM)
                keys[own_rows, columns] = normed[:ROWS]
                keys[near_rows, columns] = normed[ROWS:]
            return carry

        def project_v(chunk, carry):
            base = pl.multiple_of(chunk * CHUNK, CHUNK)
            product = jnp.dot(
                modulated[...], wq[:, pl.ds(2 * INNER + base, CHUNK)], preferred_element_type=jnp.float32
            ).astype(jnp.bfloat16)
            fresh[slot, :, pl.ds(INNER + base, CHUNK)] = product[:ROWS]
            values[own_rows, pl.ds(base, CHUNK)] = product[:ROWS]
            values[near_rows, pl.ds(base, CHUNK)] = product[ROWS:]
            return carry

        lax.fori_loop(0, INNER // CHUNK, project_q, 0)
        lax.fori_loop(0, INNER // CHUNK, project_k, 0)
        lax.fori_loop(0, INNER // CHUNK, project_v, 0)
        pltpu.make_async_copy(fresh.at[slot], kv_h.at[slot], store_sem.at[0, slot]).start()

        patch = order_s[slot]
        masks = [
            pattern_s[patch, half * PATCHES + order_s[j]].astype(jnp.float32) for half in range(2) for j in range(PATCHES)
        ]

        def attend(head, carry):
            columns = pl.ds(pl.multiple_of(head * HDIM, HDIM), HDIM)
            scores = lax.dot_general(
                queries[:, columns], keys[:, columns], (((1,), (1,)), ((), ())), preferred_element_type=jnp.float32
            )
            tiles = [
                jnp.exp2(scores[:, j * ROWS:(j + 1) * ROWS] * SCORE_SCALE) * masks[j] for j in range(2 * PATCHES)
            ]
            total = tiles[0]
            for tile in tiles[1:]:
                total = total + tile
            weight_sum = jnp.sum(total, axis=-1, keepdims=True)
            probs = jnp.concatenate([tile.astype(jnp.bfloat16) for tile in tiles], axis=1)
            mixture = jnp.dot(probs, values[:, columns], preferred_element_type=jnp.float32)
            attended[:, columns] = (mixture / weight_sum).astype(jnp.bfloat16)
            return carry

        lax.fori_loop(0, HEADS, attend, 0, unroll=4)

        def project_out(chunk, carry):
            columns = pl.ds(pl.multiple_of(chunk * CHUNK, CHUNK), CHUNK)
            product = jnp.dot(attended[...], wo[:, columns], preferred_element_type=jnp.float32)
            out_rows[slot, :, columns] = (
                x_own[slot, :, columns].astype(jnp.float32) + mod_own[pl.ds(4 * slot + 2, 1), columns] * product
            ).astype(jnp.bfloat16)
            return carry

        @pl.when(jnp.logical_and(sec < HELPED, slot == 0))
        def _():
            for i in range(NBLK - 1):
                helped_out.arrived(lax.rem(blk + 1 + i, NBLK))

        lax.fori_loop(0, D // CHUNK, project_out, 0)

        @pl.when(sec < NSEC - 1)
        def _():
            for target, landing, tx, rx in ((blk, x_own, tx_own, rx_own), (after, x_near, tx_near, rx_near)):
                pltpu.make_async_remote_copy(
                    src_ref=out_rows.at[slot], dst_ref=landing.at[slot], send_sem=tx.at[slot], recv_sem=rx.at[slot],
                    device_id=(up, target), device_id_type=MESH,
                ).start()

        pltpu.make_async_copy(out_rows.at[slot], out_h.at[slot], store_sem.at[1, slot]).start()
        return carry

    @pl.when(sec == 0)
    def _():
        for slot in range(PATCHES):
            near_copy(slot).wait_send()

    lax.fori_loop(0, PATCHES, slot_step, 0)

    qkv_main.wait_sends()
    qkv_side.wait_sends()

    @pl.when(sec >= HELPED)
    def _():
        out_main.wait_sends()
        out_side.wait_sends()

    pl.when(sec >= HELPERS)(help_out.wait_sends)
    pl.when(sec < HELPED)(helped_out.wait_sends)

    for slot in range(PATCHES):
        pltpu.make_async_copy(fresh.at[slot], kv_h.at[slot], store_sem.at[0, slot]).wait()
        pltpu.make_async_copy(out_rows.at[slot], out_h.at[slot], store_sem.at[1, slot]).wait()

    @pl.when(sec < NSEC - 1)
    def _():
        for slot in range(PATCHES):
            for tx in (tx_own, tx_near):
                pltpu.make_async_remote_copy(
                    src_ref=out_rows.at[slot], dst_ref=x_own.at[slot], send_sem=tx.at[slot], recv_sem=rx_own.at[slot],
                    device_id=(up, blk), device_id_type=MESH,
                ).wait_send()


def to_patch_order(order_s, rows_in, kv_in, rows_out, kv_out):
    rows_out[...] = rows_in[...]
    kv_out[...] = kv_in[...]


def on_device(hidden, stale_kv, w_qkv, w_out, q_gain, k_gain, mod_table, pattern, step_index, order):
    vmem, smem, anywhere = (
        pl.BlockSpec(memory_space=pltpu.VMEM),
        pl.BlockSpec(memory_space=pltpu.SMEM),
        pl.BlockSpec(memory_space=pl.ANY),
    )
    bf16, f32 = jnp.bfloat16, jnp.float32
    dma = pltpu.SemaphoreType.DMA
    rows_slots, kv_slots = pl.pallas_call(
        kernel,
        out_shape=(
            jax.ShapeDtypeStruct((PATCHES, ROWS, D), bf16),
            jax.ShapeDtypeStruct((PATCHES, ROWS, 2 * INNER), bf16),
        ),
        in_specs=[smem] * 3 + [anywhere] * 4 + [vmem] * 3,
        out_specs=(anywhere, anywhere),
        scratch_shapes=[
            pltpu.VMEM((D, 3 * INNER), bf16),
            pltpu.VMEM((INNER, D), bf16),
            pltpu.VMEM((INNER, D), bf16),
            pltpu.VMEM((2 * SEQ_DEV, INNER), bf16),
            pltpu.VMEM((2 * SEQ_DEV, INNER), bf16),
            pltpu.VMEM((PATCHES, ROWS, D), bf16),
            pltpu.VMEM((PATCHES, ROWS, D), bf16),
            pltpu.VMEM((4 * PATCHES, D), f32),
            pltpu.VMEM((4 * PATCHES, D), f32),
            pltpu.VMEM((PATCHES, ROWS, 2 * INNER), bf16),
            pltpu.VMEM((PATCHES, ROWS, D), bf16),
            pltpu.VMEM((PATCHES, ROWS, 2 * INNER), bf16),
            pltpu.VMEM((PATCHES, ROWS, D), bf16),
            pltpu.VMEM((2 * ROWS, D), bf16),
            pltpu.VMEM((ROWS, INNER), bf16),
            pltpu.VMEM((ROWS, INNER), bf16),
            dma((NBLK,)),
            dma((NBLK,)),
            dma((NBLK,)),
            dma((NBLK,)),
            dma((NBLK,)),
            dma((31,)),
            dma((31,)),
            dma((31,)),
            dma((31,)),
            dma((62,)),
            dma((1,)),
            dma((4,)),
            dma((PATCHES,)),
            dma((PATCHES,)),
            dma((PATCHES,)),
            dma((PATCHES,)),
            dma((2, PATCHES)),
            dma((2, PATCHES)),
            dma((2, PATCHES)),
            dma(()),
            dma(()),
        ],
        compiler_params=pltpu.CompilerParams(
            collective_id=0, has_side_effects=True, vmem_limit_bytes=63 * 1024 * 1024
        ),
        name="pipeline",
    )(
        order, step_index, pattern,
        hidden.reshape(PATCHES, ROWS, D), stale_kv.reshape(PATCHES, ROWS, 2 * INNER), w_qkv[0], w_out[0],
        q_gain, k_gain, mod_table.reshape(TSTEPS * 3, D),
    )

    def slot_of(patch, order_ref):
        slot = jnp.int32(0)
        for index in range(1, PATCHES):
            slot = jnp.where(order_ref[index] == patch, index, slot)
        return (slot, 0, 0)

    layer_out, kv_cache = pl.pallas_call(
        to_patch_order,
        out_shape=(
            jax.ShapeDtypeStruct((PATCHES, ROWS, D), bf16),
            jax.ShapeDtypeStruct((PATCHES, ROWS, 2 * INNER), bf16),
        ),
        grid_spec=pltpu.PrefetchScalarGridSpec(
            num_scalar_prefetch=1,
            grid=(PATCHES,),
            in_specs=[pl.BlockSpec((1, ROWS, D), slot_of), pl.BlockSpec((1, ROWS, 2 * INNER), slot_of)],
            out_specs=[
                pl.BlockSpec((1, ROWS, D), lambda patch, order_ref: (patch, 0, 0)),
                pl.BlockSpec((1, ROWS, 2 * INNER), lambda patch, order_ref: (patch, 0, 0)),
            ],
        ),
        name="patch_order",
    )(order, rows_slots, kv_slots)
    return (layer_out.reshape(1, SEQ_DEV, D), kv_cache.reshape(1, SEQ_DEV, 2 * INNER))


def solution(mesh):
    in_specs = (
        P("blk", None),
        P("section", "blk", None),
        P("section", "blk", None),
        P("section", "blk", None),
        P("section", None),
        P("section", None),
        P("section", None, None, None),
        P("blk", None),
        P("blk"),
        P(),
    )
    out_specs = (P("section", "blk", None), P("section", "blk", None))
    return jax.shard_map(
        on_device, mesh=mesh, in_specs=in_specs, out_specs=out_specs, check_vma=False
    )
```

```python
import math

import jax
import jax.numpy as jnp
from jax import lax
from jax.experimental import pallas as pl
from jax.experimental.pallas import tpu as pltpu
from jax.sharding import PartitionSpec as P

MESH = pl.DeviceIdType.MESH

D = 1536
HEADS = 12
HDIM = 128
PATCHES = 4
TSTEPS = 16
ROWS = 128
SEQ_DEV = PATCHES * ROWS
INNER = HEADS * HDIM
NY, NZ = 4, 8
NBLK = NY * NZ
NSEC = 8
SHARD = D // NBLK
NORM_EPS = 1e-06
CHUNK = 768
CHUNKS = INNER // CHUNK
SPLIT_QKV, SPLIT_OUT = 2560, 1024
OFFSETS = (0, 1, -1, 2, -2, 3, 4, 5)
FAR_UP, FAR_DOWN = 5, 2
PARTWAY = 2
HELPED = 2
HELPERS = NSEC - HELPED
SCORE_SCALE = math.log2(math.e) / math.sqrt(HDIM)


def head_norm(values, gain_row):
    square = jnp.mean(values * values, axis=-1, keepdims=True)
    return values * lax.rsqrt(square + NORM_EPS) * gain_row


def modulate(rows, scale, shift):
    values = rows.astype(jnp.float32)
    centre = values - jnp.mean(values, axis=-1, keepdims=True)
    spread = jnp.mean(centre * centre, axis=-1, keepdims=True)
    return (centre * lax.rsqrt(spread + NORM_EPS) * (1.0 + scale) + shift).astype(jnp.bfloat16)


def kernel(
    order_s, step_s, pattern_s, hidden_h, stale_h, wq_h, wo_h, qgain, kgain, mod_table,
    out_h, kv_h,
    wq, wo, wo_help, keys, values, x_own, x_near, mod_own, mod_near, stale, hidden, fresh, out_rows, modulated, queries, attended, relay,
    recv_a, recv_b, recv_o, recv_p, recv_h, send_a, send_b, send_o, send_p, send_h, send_x, local, rx_own, rx_near, tx_own, tx_near, tx_next, go, store_sem, rx_stale, tx_stale, rx_relay, tx_relay, rx_mod, tx_mod,
):
    sec = lax.axis_index("section")
    blk = lax.axis_index("blk")
    y, z = blk // NZ, lax.rem(blk, NZ)

    def at(yy, zz):
        return lax.rem(yy + 2 * NY, NY) * NZ + lax.rem(zz + 2 * NZ, NZ)

    up, down = lax.rem(sec + 1, NSEC), lax.rem(sec + NSEC - 1, NSEC)
    after, before = lax.rem(blk + 1, NBLK), lax.rem(blk + NBLK - 1, NBLK)
    chip_up, chip_down = lax.rem(sec + 2, NSEC), lax.rem(sec + NSEC - 2, NSEC)
    zp, zm, yp, ym = at(y, z + 1), at(y, z - 1), at(y + 1, z), at(y - 1, z)

    load_hidden = pltpu.make_async_copy(hidden_h, hidden, local.at[0])
    load_stale = pltpu.make_async_copy(stale_h, stale, local.at[1])
    load_wq = pltpu.make_async_copy(wq_h, wq.at[pl.ds(blk * SHARD, SHARD)], local.at[2])
    load_wo = pltpu.make_async_copy(wo_h, wo.at[pl.ds(blk * SHARD, SHARD)], local.at[3])
    load_stale.start()
    load_hidden.start()
    load_wq.start()
    load_wo.start()

    barrier = pltpu.get_barrier_semaphore()
    for target in (
        (sec, zp), (sec, zm), (sec, yp), (sec, ym), (sec, after), (sec, before),
        (up, blk), (down, blk), (up, after), (down, before), (chip_up, blk), (chip_down, blk),
    ):
        pl.semaphore_signal(barrier, inc=1, device_id=target, device_id_type=MESH)
    pl.semaphore_wait(barrier, 12)


    class Gather:
        def __init__(self, buffer, start, stop, recv, send, source):
            self.buffer, self.columns = buffer, pl.ds(start, stop - start)
            self.recv, self.send, self.source = recv, send, source
            self.count = 0

        def rows(self, shard):
            return self.buffer.at[pl.ds(pl.multiple_of(shard * SHARD, 16), SHARD), self.columns]

        def push(self, shard, *targets, from_input=False, to=None):
            for target in targets:
                copy = pltpu.make_async_remote_copy(
                    src_ref=self.source.at[:, self.columns] if from_input else self.rows(shard),
                    dst_ref=(self if to is None else to).rows(shard),
                    send_sem=self.send.at[self.count],
                    recv_sem=(self if to is None else to).recv.at[shard],
                    device_id=target if isinstance(target, tuple) else (sec, target),
                    device_id_type=MESH,
                )
                copy.start()
                self.count += 1

        def arrived(self, shard):
            pltpu.make_async_remote_copy(
                src_ref=self.rows(shard), dst_ref=self.rows(shard), send_sem=self.send.at[0],
                recv_sem=self.recv.at[shard], device_id=(up, blk), device_id_type=MESH,
            ).wait_recv()

        def along(self, shard, k):
            if OFFSETS[k] == 0:
                self.push(shard, zp, zm)
            elif 0 < OFFSETS[k] < FAR_UP:
                self.push(shard, zm)
            elif -FAR_DOWN < OFFSETS[k] < 0:
                self.push(shard, zp)

        def cross(self, k, level):
            zk = z + OFFSETS[k]
            here, there = at(y - 1, zk), at(y + 1, zk)
            self.arrived(here)
            self.arrived(there)
            if level:
                odd = lax.rem(zk + 2 * NZ, 2) == 1
                self.push(jnp.where(odd, there, here), jnp.where(odd, ym, yp))
            else:
                self.push(there, ym)
            return here, there

        def wait_sends(self):
            for index in range(self.count):
                pltpu.make_async_remote_copy(
                    src_ref=self.rows(blk), dst_ref=self.rows(blk), send_sem=self.send.at[index],
                    recv_sem=self.recv.at[blk], device_id=(up, blk), device_id_type=MESH,
                ).wait_send()

    def gather(main, side, level, between=lambda k: None):
        side.arrived(ym)
        side.arrived(yp)
        if level:
            even = lax.rem(z, 2) == 0
            side.push(jnp.where(even, ym, yp), jnp.where(even, yp, ym))
        else:
            side.push(yp, ym)
        side.push(ym, zp, zm)
        side.push(yp, zp, zm)
        for k in range(1, NZ):
            shard = at(y, z + OFFSETS[k])
            main.arrived(shard)
            main.along(shard, k)
            main.push(shard, yp, ym)
            if k == 1:
                side.arrived(at(y + 2, z))
                side.push(at(y + 2, z), zp, zm)
            main.cross(k - 1, level)
            for i in range(NY):
                shard = at(y + i, z + OFFSETS[k])
                side.arrived(shard)
                side.along(shard, k)
            between(k)
        main.cross(NZ - 1, level)
        for k in range(NZ):
            main.arrived(at(y + 2, z + OFFSETS[k]))

    qkv_main = Gather(wq, 0, SPLIT_QKV, recv_a, send_a, wq_h)
    qkv_side = Gather(wq, SPLIT_QKV, 3 * INNER, recv_b, send_b, wq_h)
    out_main = Gather(wo, 0, SPLIT_OUT, recv_o, send_o, wo_h)
    out_side = Gather(wo, SPLIT_OUT, D, recv_p, send_p, wo_h)
    help_out = Gather(wo_help, 0, D, recv_h, send_h, wo_h)
    helped_out = Gather(wo, 0, D, recv_o, send_x, wo_h)

    @pl.when(sec < HELPED)
    def _():
        helped_out.push(blk, (chip_down, blk), from_input=True, to=help_out)

    is_even = lax.rem(sec, 2) == 0

    def let_go():
        pl.semaphore_signal(go, inc=1, device_id=(up, blk), device_id_type=MESH)

    @pl.when(jnp.logical_not(is_even))
    def _():
        pl.semaphore_wait(go, 1)

    @pl.when(sec >= HELPERS)
    def _():
        for k in range(NZ):
            shard = at(y, z + OFFSETS[k])
            help_out.arrived(shard)
            help_out.along(shard, k)
            help_out.push(shard, yp, ym)
            if k > 0:
                help_out.push(shard, (chip_up, blk), to=helped_out)
                for shard in help_out.cross(k - 1, True):
                    help_out.push(shard, (chip_up, blk), to=helped_out)
            if k > 1:
                shard = at(y + 2, z + OFFSETS[k - 2])
                help_out.arrived(shard)
                help_out.push(shard, (chip_up, blk), to=helped_out)
        for shard in help_out.cross(NZ - 1, True):
            help_out.push(shard, (chip_up, blk), to=helped_out)
        for k in (NZ - 2, NZ - 1):
            shard = at(y + 2, z + OFFSETS[k])
            help_out.arrived(shard)
            help_out.push(shard, (chip_up, blk), to=helped_out)

    pl.when(sec == HELPERS)(let_go)
    qkv_side.push(blk, yp, ym, from_input=True)
    qkv_main.push(blk, zp, zm, yp, ym, from_input=True)
    qkv_side.push(blk, zp, zm, from_input=True)

    for slot in range(PATCHES):
        step = step_s[order_s[slot]]
        for row in range(3):
            mod_own[pl.ds(4 * slot + row, 1), :] = mod_table[pl.ds(3 * step + row, 1), :]
    send_mod = pltpu.make_async_remote_copy(
        src_ref=mod_own, dst_ref=mod_near, send_sem=tx_mod, recv_sem=rx_mod,
        device_id=(sec, after), device_id_type=MESH,
    )
    send_mod.start()

    load_hidden.wait()

    def near_copy(slot, chunk):
        columns = pl.ds(chunk * CHUNK, CHUNK)
        return pltpu.make_async_remote_copy(
            src_ref=x_own.at[slot, :, columns], dst_ref=x_near.at[slot, :, columns],
            send_sem=tx_near.at[slot, chunk], recv_sem=rx_near.at[slot, chunk],
            device_id=(sec, after), device_id_type=MESH,
        )

    def next_copy(slot, chunk, near):
        columns = pl.ds(pl.multiple_of(chunk * CHUNK, CHUNK), CHUNK)
        landing, tx, rx, target = (x_near, tx_next, rx_near, after) if near else (x_own, tx_own, rx_own, blk)
        return pltpu.make_async_remote_copy(
            src_ref=out_rows.at[slot, :, columns], dst_ref=landing.at[slot, :, columns],
            send_sem=tx.at[slot, chunk], recv_sem=rx.at[slot, chunk],
            device_id=(up, target), device_id_type=MESH,
        )

    @pl.when(sec == 0)
    def _():
        for slot in range(PATCHES):
            x_own[slot] = hidden[order_s[slot]]
        for chunk in range(CHUNKS):
            near_copy(0, chunk).start()

    load_stale.wait()
    for slot in range(1, PATCHES):
        patch = order_s[slot]
        for head in range(HEADS):
            columns = pl.ds(head * HDIM, HDIM)
            keys[pl.ds(slot * ROWS, ROWS), columns] = head_norm(
                stale[patch, :, columns].astype(jnp.float32), kgain[...]
            ).astype(jnp.bfloat16)
        values[pl.ds(slot * ROWS, ROWS), :] = stale[patch, :, INNER:]
    pieces = 2 * (PATCHES - 1)
    by_relay = jnp.logical_and(jnp.logical_not(is_even), z == NZ - 1)

    def stale_rows(i, half):
        buffer = (keys, values)[i % 2]
        return buffer.at[pl.ds(half * SEQ_DEV + (i // 2 + 1) * ROWS, ROWS)]

    def stale_copy(i):
        return pltpu.make_async_remote_copy(
            src_ref=stale_rows(i, 0), dst_ref=stale_rows(i, 1), send_sem=tx_stale.at[i], recv_sem=rx_stale.at[i],
            device_id=(sec, after), device_id_type=MESH,
        )

    def relay_copy(i, second):
        return pltpu.make_async_remote_copy(
            src_ref=relay.at[i] if second else stale_rows(i, 0),
            dst_ref=stale_rows(i, 1) if second else relay.at[i],
            send_sem=(tx_relay if second else tx_stale).at[i],
            recv_sem=(rx_stale if second else rx_relay).at[i],
            device_id=(sec, zp if second else yp), device_id_type=MESH,
        )

    def between(k):
        if 1 <= k <= pieces:
            @pl.when(by_relay)
            def _():
                relay_copy(k - 1, False).start()

            @pl.when(jnp.logical_not(by_relay))
            def _():
                stale_copy(k - 1).start()

        if 3 <= k < pieces + 3:
            @pl.when(by_relay)
            def _():
                relay_copy(k - 3, False).wait_recv()
                relay_copy(k - 3, True).start()

        if k == PARTWAY:
            pl.when(jnp.logical_and(is_even, sec < HELPERS))(let_go)

    gather(qkv_main, qkv_side, False, between)
    between(NZ)

    @pl.when(sec == 0)
    def _():
        for slot in range(1, PATCHES):
            for chunk in range(CHUNKS):
                near_copy(slot, chunk).start()

    @pl.when(sec >= HELPED)
    def _():
        out_side.push(blk, yp, ym, from_input=True)
        out_main.push(blk, zp, zm, yp, ym, from_input=True)
        out_side.push(blk, zp, zm, from_input=True)
        gather(out_main, out_side, True)

    load_wq.wait()
    load_wo.wait()
    send_mod.wait()
    for i in range(pieces):
        stale_copy(i).wait()

    @pl.when(by_relay)
    def _():
        for i in range(pieces):
            relay_copy(i, True).wait_send()

    def slot_step(slot, carry):
        @pl.when(sec > 0)
        def _():
            for chunk in range(CHUNKS):
                next_copy(slot, chunk, False).wait_recv()

                @pl.when(is_even)
                def _():
                    near_copy(slot, chunk).start()

        modulated[pl.ds(0, ROWS), :] = modulate(
            x_own[slot], mod_own[pl.ds(4 * slot + 1, 1), :], mod_own[pl.ds(4 * slot, 1), :]
        )
        own_rows = pl.ds(pl.multiple_of(slot * ROWS, ROWS), ROWS)
        near_rows = pl.ds(pl.multiple_of(SEQ_DEV + slot * ROWS, ROWS), ROWS)

        def project_q(chunk, carry):
            base = pl.multiple_of(chunk * CHUNK, CHUNK)
            product = jnp.dot(
                modulated[pl.ds(0, ROWS), :], wq[:, pl.ds(base, CHUNK)], preferred_element_type=jnp.float32
            )
            for head in range(CHUNK // HDIM):
                queries[:, pl.ds(base + head * HDIM, HDIM)] = head_norm(
                    product[:, head * HDIM:(head + 1) * HDIM], qgain[...]
                ).astype(jnp.bfloat16)
            return carry

        def project_k(chunk, carry):
            base = pl.multiple_of(chunk * CHUNK, CHUNK)
            product = jnp.dot(
                modulated[...], wq[:, pl.ds(INNER + base, CHUNK)], preferred_element_type=jnp.float32
            ).astype(jnp.bfloat16)
            fresh[slot, :, pl.ds(base, CHUNK)] = product[:ROWS]
            for head in range(CHUNK // HDIM):
                normed = head_norm(
                    product[:, head * HDIM:(head + 1) * HDIM].astype(jnp.float32), kgain[...]
                ).astype(jnp.bfloat16)
                columns = pl.ds(base + head * HDIM, HDIM)
                keys[own_rows, columns] = normed[:ROWS]
                keys[near_rows, columns] = normed[ROWS:]
            return carry

        def project_v(chunk, carry):
            base = pl.multiple_of(chunk * CHUNK, CHUNK)
            product = jnp.dot(
                modulated[...], wq[:, pl.ds(2 * INNER + base, CHUNK)], preferred_element_type=jnp.float32
            ).astype(jnp.bfloat16)
            fresh[slot, :, pl.ds(INNER + base, CHUNK)] = product[:ROWS]
            values[own_rows, pl.ds(base, CHUNK)] = product[:ROWS]
            values[near_rows, pl.ds(base, CHUNK)] = product[ROWS:]
            return carry

        lax.fori_loop(0, CHUNKS, project_q, 0)
        for chunk in range(CHUNKS):
            near_copy(slot, chunk).wait_recv()
        modulated[pl.ds(ROWS, ROWS), :] = modulate(
            x_near[slot], mod_near[pl.ds(4 * slot + 1, 1), :], mod_near[pl.ds(4 * slot, 1), :]
        )
        lax.fori_loop(0, CHUNKS, project_k, 0)
        lax.fori_loop(0, CHUNKS, project_v, 0)
        pltpu.make_async_copy(fresh.at[slot], kv_h.at[slot], store_sem.at[0, slot]).start()

        patch = order_s[slot]
        masks = [
            pattern_s[patch, half * PATCHES + order_s[j]].astype(jnp.float32) for half in range(2) for j in range(PATCHES)
        ]

        def attend(head, carry):
            columns = pl.ds(pl.multiple_of(head * HDIM, HDIM), HDIM)
            scores = lax.dot_general(
                queries[:, columns], keys[:, columns], (((1,), (1,)), ((), ())), preferred_element_type=jnp.float32
            )
            tiles = [
                jnp.exp2(scores[:, j * ROWS:(j + 1) * ROWS] * SCORE_SCALE) * masks[j] for j in range(2 * PATCHES)
            ]
            total = tiles[0]
            for tile in tiles[1:]:
                total = total + tile
            weight_sum = jnp.sum(total, axis=-1, keepdims=True)
            probs = jnp.concatenate([tile.astype(jnp.bfloat16) for tile in tiles], axis=1)
            mixture = jnp.dot(probs, values[:, columns], preferred_element_type=jnp.float32)
            attended[:, columns] = (mixture / weight_sum).astype(jnp.bfloat16)
            return carry

        lax.fori_loop(0, HEADS, attend, 0, unroll=4)

        def project_out(chunk, carry):
            columns = pl.ds(pl.multiple_of(chunk * CHUNK, CHUNK), CHUNK)
            product = jnp.dot(attended[...], wo[:, columns], preferred_element_type=jnp.float32)
            out_rows[slot, :, columns] = (
                x_own[slot, :, columns].astype(jnp.float32) + mod_own[pl.ds(4 * slot + 2, 1), columns] * product
            ).astype(jnp.bfloat16)

            @pl.when(sec < NSEC - 1)
            def _():
                next_copy(slot, chunk, False).start()

                @pl.when(is_even)
                def _():
                    next_copy(slot, chunk, True).start()

            return carry

        @pl.when(jnp.logical_and(sec < HELPED, slot == 0))
        def _():
            for i in range(NBLK - 1):
                helped_out.arrived(lax.rem(blk + 1 + i, NBLK))

        lax.fori_loop(0, CHUNKS, project_out, 0)

        pltpu.make_async_copy(out_rows.at[slot], out_h.at[slot], store_sem.at[1, slot]).start()
        return carry

    lax.fori_loop(0, PATCHES, slot_step, 0)

    qkv_main.wait_sends()
    qkv_side.wait_sends()

    @pl.when(sec >= HELPED)
    def _():
        out_main.wait_sends()
        out_side.wait_sends()

    pl.when(sec >= HELPERS)(help_out.wait_sends)
    pl.when(sec < HELPED)(helped_out.wait_sends)

    for slot in range(PATCHES):
        pltpu.make_async_copy(fresh.at[slot], kv_h.at[slot], store_sem.at[0, slot]).wait()
        pltpu.make_async_copy(out_rows.at[slot], out_h.at[slot], store_sem.at[1, slot]).wait()

    @pl.when(is_even)
    def _():
        for slot in range(PATCHES):
            for chunk in range(CHUNKS):
                near_copy(slot, chunk).wait_send()
                next_copy(slot, chunk, True).wait_send()

    @pl.when(sec < NSEC - 1)
    def _():
        for slot in range(PATCHES):
            for chunk in range(CHUNKS):
                next_copy(slot, chunk, False).wait_send()


def to_patch_order(order_s, rows_in, kv_in, rows_out, kv_out):
    rows_out[...] = rows_in[...]
    kv_out[...] = kv_in[...]


def on_device(hidden, stale_kv, w_qkv, w_out, q_gain, k_gain, mod_table, pattern, step_index, order):
    vmem, smem, anywhere = (
        pl.BlockSpec(memory_space=pltpu.VMEM),
        pl.BlockSpec(memory_space=pltpu.SMEM),
        pl.BlockSpec(memory_space=pl.ANY),
    )
    bf16, f32 = jnp.bfloat16, jnp.float32
    dma = pltpu.SemaphoreType.DMA
    rows_slots, kv_slots = pl.pallas_call(
        kernel,
        out_shape=(
            jax.ShapeDtypeStruct((PATCHES, ROWS, D), bf16),
            jax.ShapeDtypeStruct((PATCHES, ROWS, 2 * INNER), bf16),
        ),
        in_specs=[smem] * 3 + [anywhere] * 4 + [vmem] * 3,
        out_specs=(anywhere, anywhere),
        scratch_shapes=[
            pltpu.VMEM((D, 3 * INNER), bf16),
            pltpu.VMEM((INNER, D), bf16),
            pltpu.VMEM((INNER, D), bf16),
            pltpu.VMEM((2 * SEQ_DEV, INNER), bf16),
            pltpu.VMEM((2 * SEQ_DEV, INNER), bf16),
            pltpu.VMEM((PATCHES, ROWS, D), bf16),
            pltpu.VMEM((PATCHES, ROWS, D), bf16),
            pltpu.VMEM((4 * PATCHES, D), f32),
            pltpu.VMEM((4 * PATCHES, D), f32),
            pltpu.VMEM((PATCHES, ROWS, 2 * INNER), bf16),
            pltpu.VMEM((PATCHES, ROWS, D), bf16),
            pltpu.VMEM((PATCHES, ROWS, 2 * INNER), bf16),
            pltpu.VMEM((PATCHES, ROWS, D), bf16),
            pltpu.VMEM((2 * ROWS, D), bf16),
            pltpu.VMEM((ROWS, INNER), bf16),
            pltpu.VMEM((ROWS, INNER), bf16),
            pltpu.VMEM((2 * (PATCHES - 1), ROWS, INNER), bf16),
            dma((NBLK,)),
            dma((NBLK,)),
            dma((NBLK,)),
            dma((NBLK,)),
            dma((NBLK,)),
            dma((31,)),
            dma((31,)),
            dma((31,)),
            dma((31,)),
            dma((62,)),
            dma((1,)),
            dma((4,)),
            dma((PATCHES, CHUNKS)),
            dma((PATCHES, CHUNKS)),
            dma((PATCHES, CHUNKS)),
            dma((PATCHES, CHUNKS)),
            dma((PATCHES, CHUNKS)),
            pltpu.SemaphoreType.REGULAR,
            dma((2, PATCHES)),
            dma((2 * (PATCHES - 1),)),
            dma((2 * (PATCHES - 1),)),
            dma((2 * (PATCHES - 1),)),
            dma((2 * (PATCHES - 1),)),
            dma(()),
            dma(()),
        ],
        compiler_params=pltpu.CompilerParams(
            collective_id=0, has_side_effects=True, vmem_limit_bytes=63 * 1024 * 1024
        ),
        name="pipeline",
    )(
        order, step_index, pattern,
        hidden.reshape(PATCHES, ROWS, D), stale_kv.reshape(PATCHES, ROWS, 2 * INNER), w_qkv[0], w_out[0],
        q_gain, k_gain, mod_table.reshape(TSTEPS * 3, D),
    )

    def slot_of(patch, order_ref):
        slot = jnp.int32(0)
        for index in range(1, PATCHES):
            slot = jnp.where(order_ref[index] == patch, index, slot)
        return (slot, 0, 0)

    layer_out, kv_cache = pl.pallas_call(
        to_patch_order,
        out_shape=(
            jax.ShapeDtypeStruct((PATCHES, ROWS, D), bf16),
            jax.ShapeDtypeStruct((PATCHES, ROWS, 2 * INNER), bf16),
        ),
        grid_spec=pltpu.PrefetchScalarGridSpec(
            num_scalar_prefetch=1,
            grid=(PATCHES,),
            in_specs=[pl.BlockSpec((1, ROWS, D), slot_of), pl.BlockSpec((1, ROWS, 2 * INNER), slot_of)],
            out_specs=[
                pl.BlockSpec((1, ROWS, D), lambda patch, order_ref: (patch, 0, 0)),
                pl.BlockSpec((1, ROWS, 2 * INNER), lambda patch, order_ref: (patch, 0, 0)),
            ],
        ),
        name="patch_order",
    )(order, rows_slots, kv_slots)
    return (layer_out.reshape(1, SEQ_DEV, D), kv_cache.reshape(1, SEQ_DEV, 2 * INNER))


def solution(mesh):
    in_specs = (
        P("blk", None),
        P("section", "blk", None),
        P("section", "blk", None),
        P("section", "blk", None),
        P("section", None),
        P("section", None),
        P("section", None, None, None),
        P("blk", None),
        P("blk"),
        P(),
    )
    out_specs = (P("section", "blk", None), P("section", "blk", None))
    return jax.shard_map(
        on_device, mesh=mesh, in_specs=in_specs, out_specs=out_specs, check_vma=False
    )
```

```python
import functools
import math

import jax
import jax.numpy as jnp
from jax import lax
from jax.experimental import pallas as pl
from jax.experimental.pallas import tpu as pltpu
from jax.sharding import PartitionSpec as P

MESH = pl.DeviceIdType.MESH

D = 1536
HEADS = 12
HDIM = 128
PATCHES = 4
TSTEPS = 16
ROWS = 128
SEQ_DEV = PATCHES * ROWS
INNER = HEADS * HDIM
NY, NZ = 4, 8
NBLK = NY * NZ
NSEC = 8
SHARD = D // NBLK
NORM_EPS = 1e-06
CHUNK = 768
CHUNKS = INNER // CHUNK
SPLIT = 2560
OFFSETS = (0, 1, -1, 2, -2, 3, 4, 5)
FAR_UP, FAR_DOWN = 5, 2
PARTWAY = 2
LAG = 1
HELPED = 2
HELPERS = NSEC - HELPED
SCORE_SCALE = math.log2(math.e) / math.sqrt(HDIM)


def head_norm(values, gain_row):
    square = jnp.mean(values * values, axis=-1, keepdims=True)
    return values * lax.rsqrt(square + NORM_EPS) * gain_row


def modulate(rows, scale, shift):
    values = rows.astype(jnp.float32)
    centre = values - jnp.mean(values, axis=-1, keepdims=True)
    spread = jnp.mean(centre * centre, axis=-1, keepdims=True)
    return (centre * lax.rsqrt(spread + NORM_EPS) * (1.0 + scale) + shift).astype(jnp.bfloat16)


def kernel(
    order_s, step_s, pattern_s, hidden_h, stale_h, wq_h, wo_h, qgain, kgain, mod_table,
    out_h, kv_h,
    wq, wo, wo_help, keys, values, x_own, x_near, mod_own, mod_near, stale, hidden, fresh, out_rows, modulated, queries, attended, relay,
    recv_a, recv_b, recv_o, recv_h, send_a, send_b, send_o, send_h, send_x, local, rx_own, rx_near, tx_own, tx_near, tx_next, go, store_sem, rx_stale, tx_stale, rx_relay, tx_relay, rx_mod, tx_mod,
):
    sec = lax.axis_index("section")
    blk = lax.axis_index("blk")
    y, z = blk // NZ, lax.rem(blk, NZ)

    def at(yy, zz):
        return lax.rem(yy + 2 * NY, NY) * NZ + lax.rem(zz + 2 * NZ, NZ)

    up, down = lax.rem(sec + 1, NSEC), lax.rem(sec + NSEC - 1, NSEC)
    after, before = lax.rem(blk + 1, NBLK), lax.rem(blk + NBLK - 1, NBLK)
    chip_up, chip_down = lax.rem(sec + 2, NSEC), lax.rem(sec + NSEC - 2, NSEC)
    zp, zm, yp, ym = at(y, z + 1), at(y, z - 1), at(y + 1, z), at(y - 1, z)

    load_hidden = pltpu.make_async_copy(hidden_h, hidden, local.at[0])
    load_stale = pltpu.make_async_copy(stale_h, stale, local.at[1])
    load_wq = pltpu.make_async_copy(wq_h, wq.at[pl.ds(blk * SHARD, SHARD)], local.at[2])
    load_wo = pltpu.make_async_copy(wo_h, wo.at[pl.ds(blk * SHARD, SHARD)], local.at[3])
    load_stale.start()
    load_hidden.start()
    load_wq.start()
    load_wo.start()

    barrier = pltpu.get_barrier_semaphore()
    for target in (
        (sec, zp), (sec, zm), (sec, yp), (sec, ym), (sec, after), (sec, before),
        (up, blk), (down, blk), (up, after), (down, before), (chip_up, blk), (chip_down, blk),
    ):
        pl.semaphore_signal(barrier, inc=1, device_id=target, device_id_type=MESH)
    pl.semaphore_wait(barrier, 12)


    class Gather:
        def __init__(self, buffer, start, stop, recv, send, source):
            self.buffer, self.columns = buffer, pl.ds(start, stop - start)
            self.recv, self.send, self.source = recv, send, source
            self.count = 0

        def rows(self, shard):
            return self.buffer.at[pl.ds(pl.multiple_of(shard * SHARD, 16), SHARD), self.columns]

        def push(self, shard, *targets, from_input=False, to=None):
            for target in targets:
                copy = pltpu.make_async_remote_copy(
                    src_ref=self.source.at[:, self.columns] if from_input else self.rows(shard),
                    dst_ref=(self if to is None else to).rows(shard),
                    send_sem=self.send.at[self.count],
                    recv_sem=(self if to is None else to).recv.at[shard],
                    device_id=target if isinstance(target, tuple) else (sec, target),
                    device_id_type=MESH,
                )
                copy.start()
                self.count += 1

        def arrived(self, shard):
            pltpu.make_async_remote_copy(
                src_ref=self.rows(shard), dst_ref=self.rows(shard), send_sem=self.send.at[0],
                recv_sem=self.recv.at[shard], device_id=(up, blk), device_id_type=MESH,
            ).wait_recv()

        def along(self, shard, k):
            if OFFSETS[k] == 0:
                self.push(shard, zp, zm)
            elif 0 < OFFSETS[k] < FAR_UP:
                self.push(shard, zm)
            elif -FAR_DOWN < OFFSETS[k] < 0:
                self.push(shard, zp)

        def cross(self, k, level):
            zk = z + OFFSETS[k]
            here, there = at(y - 1, zk), at(y + 1, zk)
            self.arrived(here)
            self.arrived(there)
            if level:
                odd = lax.rem(zk + 2 * NZ, 2) == 1
                self.push(jnp.where(odd, there, here), jnp.where(odd, ym, yp))
            else:
                self.push(there, ym)
            return here, there

        def ring_step(self, k):
            shard = at(y, z + OFFSETS[k])
            self.arrived(shard)
            self.along(shard, k)
            self.push(shard, yp, ym)
            if k > 0:
                self.cross(k - 1, True)

        def wait_sends(self):
            for index in range(self.count):
                pltpu.make_async_remote_copy(
                    src_ref=self.rows(blk), dst_ref=self.rows(blk), send_sem=self.send.at[index],
                    recv_sem=self.recv.at[blk], device_id=(up, blk), device_id_type=MESH,
                ).wait_send()

    main = Gather(wq, 0, SPLIT, recv_a, send_a, wq_h)
    side = Gather(wq, SPLIT, 3 * INNER, recv_b, send_b, wq_h)
    out = Gather(wo, 0, D, recv_o, send_o, wo_h)
    help_out = Gather(wo_help, 0, D, recv_h, send_h, wo_h)
    helped_out = Gather(wo, 0, D, recv_o, send_x, wo_h)

    @pl.when(sec < HELPED)
    def _():
        helped_out.push(blk, (chip_down, blk), from_input=True, to=help_out)

    is_even = lax.rem(sec, 2) == 0

    def let_go():
        pl.semaphore_signal(go, inc=1, device_id=(up, blk), device_id_type=MESH)

    @pl.when(jnp.logical_not(is_even))
    def _():
        pl.semaphore_wait(go, 1)

    @pl.when(sec >= HELPERS)
    def _():
        for k in range(NZ):
            shard = at(y, z + OFFSETS[k])
            help_out.arrived(shard)
            help_out.along(shard, k)
            help_out.push(shard, yp, ym)
            if k > 0:
                help_out.push(shard, (chip_up, blk), to=helped_out)
                for shard in help_out.cross(k - 1, True):
                    help_out.push(shard, (chip_up, blk), to=helped_out)
            if k > 1:
                shard = at(y + 2, z + OFFSETS[k - 2])
                help_out.arrived(shard)
                help_out.push(shard, (chip_up, blk), to=helped_out)
        for shard in help_out.cross(NZ - 1, True):
            help_out.push(shard, (chip_up, blk), to=helped_out)
        for k in (NZ - 2, NZ - 1):
            shard = at(y + 2, z + OFFSETS[k])
            help_out.arrived(shard)
            help_out.push(shard, (chip_up, blk), to=helped_out)

    pl.when(sec == HELPERS)(let_go)
    side.push(blk, yp, ym, from_input=True)
    main.push(blk, zp, zm, yp, ym, from_input=True)
    side.push(blk, zp, zm, from_input=True)

    @pl.when(sec >= HELPED)
    def _():
        out.push(blk, zp, zm, yp, ym, from_input=True)

    for slot in range(PATCHES):
        step = step_s[order_s[slot]]
        for row in range(3):
            mod_own[pl.ds(4 * slot + row, 1), :] = mod_table[pl.ds(3 * step + row, 1), :]
    send_mod = pltpu.make_async_remote_copy(
        src_ref=mod_own, dst_ref=mod_near, send_sem=tx_mod, recv_sem=rx_mod,
        device_id=(sec, after), device_id_type=MESH,
    )
    send_mod.start()

    load_hidden.wait()

    def near_copy(slot, chunk):
        columns = pl.ds(chunk * CHUNK, CHUNK)
        return pltpu.make_async_remote_copy(
            src_ref=x_own.at[slot, :, columns], dst_ref=x_near.at[slot, :, columns],
            send_sem=tx_near.at[slot, chunk], recv_sem=rx_near.at[slot, chunk],
            device_id=(sec, after), device_id_type=MESH,
        )

    def next_copy(slot, chunk, near):
        columns = pl.ds(pl.multiple_of(chunk * CHUNK, CHUNK), CHUNK)
        landing, tx, rx, target = (x_near, tx_next, rx_near, after) if near else (x_own, tx_own, rx_own, blk)
        return pltpu.make_async_remote_copy(
            src_ref=out_rows.at[slot, :, columns], dst_ref=landing.at[slot, :, columns],
            send_sem=tx.at[slot, chunk], recv_sem=rx.at[slot, chunk],
            device_id=(up, target), device_id_type=MESH,
        )

    @pl.when(sec == 0)
    def _():
        for slot in range(PATCHES):
            x_own[slot] = hidden[order_s[slot]]
        for chunk in range(CHUNKS):
            near_copy(0, chunk).start()

    load_stale.wait()
    for slot in range(1, PATCHES):
        patch = order_s[slot]
        for head in range(HEADS):
            columns = pl.ds(head * HDIM, HDIM)
            keys[pl.ds(slot * ROWS, ROWS), columns] = head_norm(
                stale[patch, :, columns].astype(jnp.float32), kgain[...]
            ).astype(jnp.bfloat16)
        values[pl.ds(slot * ROWS, ROWS), :] = stale[patch, :, INNER:]
    pieces = 2 * (PATCHES - 1)
    by_relay = jnp.logical_and(jnp.logical_not(is_even), z == NZ - 1)

    def stale_rows(i, half):
        buffer = (keys, values)[i % 2]
        return buffer.at[pl.ds(half * SEQ_DEV + (i // 2 + 1) * ROWS, ROWS)]

    def stale_copy(i):
        return pltpu.make_async_remote_copy(
            src_ref=stale_rows(i, 0), dst_ref=stale_rows(i, 1), send_sem=tx_stale.at[i], recv_sem=rx_stale.at[i],
            device_id=(sec, after), device_id_type=MESH,
        )

    def relay_copy(i, second):
        return pltpu.make_async_remote_copy(
            src_ref=relay.at[i] if second else stale_rows(i, 0),
            dst_ref=stale_rows(i, 1) if second else relay.at[i],
            send_sem=(tx_relay if second else tx_stale).at[i],
            recv_sem=(rx_stale if second else rx_relay).at[i],
            device_id=(sec, zp if second else yp), device_id_type=MESH,
        )

    def between(k):
        if 1 <= k <= pieces:
            @pl.when(by_relay)
            def _():
                relay_copy(k - 1, False).start()

            @pl.when(jnp.logical_not(by_relay))
            def _():
                stale_copy(k - 1).start()

        if 3 <= k < pieces + 3:
            @pl.when(by_relay)
            def _():
                relay_copy(k - 3, False).wait_recv()
                relay_copy(k - 3, True).start()

        if k == PARTWAY:
            pl.when(jnp.logical_and(is_even, sec < HELPERS))(let_go)

    side.arrived(ym)
    side.arrived(yp)
    side.push(yp, ym)
    side.push(ym, zp, zm)
    side.push(yp, zp, zm)
    for k in range(1, NZ):
        shard = at(y, z + OFFSETS[k])
        main.arrived(shard)
        main.along(shard, k)
        main.push(shard, yp, ym)
        if k == 1:
            side.arrived(at(y + 2, z))
            side.push(at(y + 2, z), zp, zm)
        main.cross(k - 1, False)
        for i in range(NY):
            shard = at(y + i, z + OFFSETS[k])
            side.arrived(shard)
            side.along(shard, k)
        between(k)
        if k > LAG:
            pl.when(sec >= HELPED)(functools.partial(out.ring_step, k - LAG))
    main.cross(NZ - 1, False)
    for k in range(NZ):
        main.arrived(at(y + 2, z + OFFSETS[k]))
    between(NZ)

    @pl.when(sec == 0)
    def _():
        for chunk in range(CHUNKS):
            near_copy(1, chunk).start()

    @pl.when(sec >= HELPED)
    def _():
        for k in range(NZ - LAG, NZ):
            out.ring_step(k)
        out.cross(NZ - 1, True)
        for k in range(NZ):
            out.arrived(at(y + 2, z + OFFSETS[k]))

    load_wq.wait()
    load_wo.wait()
    send_mod.wait()
    for i in range(pieces):
        stale_copy(i).wait()

    @pl.when(by_relay)
    def _():
        for i in range(pieces):
            relay_copy(i, True).wait_send()

    def slot_step(slot, carry):
        @pl.when(jnp.logical_and(sec == 0, slot < PATCHES - 2))
        def _():
            for chunk in range(CHUNKS):
                near_copy(slot + 2, chunk).start()

        @pl.when(sec > 0)
        def _():
            for chunk in range(CHUNKS):
                next_copy(slot, chunk, False).wait_recv()

                @pl.when(jnp.logical_and(is_even, slot == PATCHES - 1))
                def _():
                    near_copy(slot, chunk).start()

        modulated[pl.ds(0, ROWS), :] = modulate(
            x_own[slot], mod_own[pl.ds(4 * slot + 1, 1), :], mod_own[pl.ds(4 * slot, 1), :]
        )
        own_rows = pl.ds(pl.multiple_of(slot * ROWS, ROWS), ROWS)
        near_rows = pl.ds(pl.multiple_of(SEQ_DEV + slot * ROWS, ROWS), ROWS)

        def project_q(chunk, carry):
            base = pl.multiple_of(chunk * CHUNK, CHUNK)
            product = jnp.dot(
                modulated[pl.ds(0, ROWS), :], wq[:, pl.ds(base, CHUNK)], preferred_element_type=jnp.float32
            )
            for head in range(CHUNK // HDIM):
                queries[:, pl.ds(base + head * HDIM, HDIM)] = head_norm(
                    product[:, head * HDIM:(head + 1) * HDIM], qgain[...]
                ).astype(jnp.bfloat16)
            return carry

        def project_k(chunk, carry):
            base = pl.multiple_of(chunk * CHUNK, CHUNK)
            product = jnp.dot(
                modulated[...], wq[:, pl.ds(INNER + base, CHUNK)], preferred_element_type=jnp.float32
            ).astype(jnp.bfloat16)
            fresh[slot, :, pl.ds(base, CHUNK)] = product[:ROWS]
            for head in range(CHUNK // HDIM):
                normed = head_norm(
                    product[:, head * HDIM:(head + 1) * HDIM].astype(jnp.float32), kgain[...]
                ).astype(jnp.bfloat16)
                columns = pl.ds(base + head * HDIM, HDIM)
                keys[own_rows, columns] = normed[:ROWS]
                keys[near_rows, columns] = normed[ROWS:]
            return carry

        def project_v(chunk, carry):
            base = pl.multiple_of(chunk * CHUNK, CHUNK)
            product = jnp.dot(
                modulated[...], wq[:, pl.ds(2 * INNER + base, CHUNK)], preferred_element_type=jnp.float32
            ).astype(jnp.bfloat16)
            fresh[slot, :, pl.ds(INNER + base, CHUNK)] = product[:ROWS]
            values[own_rows, pl.ds(base, CHUNK)] = product[:ROWS]
            values[near_rows, pl.ds(base, CHUNK)] = product[ROWS:]
            return carry

        lax.fori_loop(0, CHUNKS, project_q, 0)
        for chunk in range(CHUNKS):
            near_copy(slot, chunk).wait_recv()
        modulated[pl.ds(ROWS, ROWS), :] = modulate(
            x_near[slot], mod_near[pl.ds(4 * slot + 1, 1), :], mod_near[pl.ds(4 * slot, 1), :]
        )
        lax.fori_loop(0, CHUNKS, project_k, 0)
        lax.fori_loop(0, CHUNKS, project_v, 0)
        pltpu.make_async_copy(fresh.at[slot], kv_h.at[slot], store_sem.at[0, slot]).start()

        patch = order_s[slot]
        masks = [
            pattern_s[patch, half * PATCHES + order_s[j]].astype(jnp.float32) for half in range(2) for j in range(PATCHES)
        ]

        def attend(head, carry):
            columns = pl.ds(pl.multiple_of(head * HDIM, HDIM), HDIM)
            scores = lax.dot_general(
                queries[:, columns], keys[:, columns], (((1,), (1,)), ((), ())), preferred_element_type=jnp.float32
            )
            tiles = [
                jnp.exp2(scores[:, j * ROWS:(j + 1) * ROWS] * SCORE_SCALE) * masks[j] for j in range(2 * PATCHES)
            ]
            total = tiles[0]
            for tile in tiles[1:]:
                total = total + tile
            weight_sum = jnp.sum(total, axis=-1, keepdims=True)
            probs = jnp.concatenate([tile.astype(jnp.bfloat16) for tile in tiles], axis=1)
            mixture = jnp.dot(probs, values[:, columns], preferred_element_type=jnp.float32)
            attended[:, columns] = (mixture / weight_sum).astype(jnp.bfloat16)
            return carry

        lax.fori_loop(0, HEADS, attend, 0, unroll=4)

        def project_out(chunk, carry):
            columns = pl.ds(pl.multiple_of(chunk * CHUNK, CHUNK), CHUNK)
            product = jnp.dot(attended[...], wo[:, columns], preferred_element_type=jnp.float32)
            out_rows[slot, :, columns] = (
                x_own[slot, :, columns].astype(jnp.float32) + mod_own[pl.ds(4 * slot + 2, 1), columns] * product
            ).astype(jnp.bfloat16)

            @pl.when(sec < NSEC - 1)
            def _():
                next_copy(slot, chunk, False).start()

                @pl.when(is_even)
                def _():
                    next_copy(slot, chunk, True).start()

            return carry

        @pl.when(jnp.logical_and(sec < HELPED, slot == 0))
        def _():
            for i in range(NBLK - 1):
                helped_out.arrived(lax.rem(blk + 1 + i, NBLK))

        lax.fori_loop(0, CHUNKS, project_out, 0)

        @pl.when(jnp.logical_and(jnp.logical_not(is_even), jnp.logical_and(sec < NSEC - 1, slot < PATCHES - 1)))
        def _():
            for chunk in range(CHUNKS):
                next_copy(slot, chunk, True).start()

        pltpu.make_async_copy(out_rows.at[slot], out_h.at[slot], store_sem.at[1, slot]).start()
        return carry

    lax.fori_loop(0, PATCHES, slot_step, 0)

    main.wait_sends()
    side.wait_sends()

    pl.when(sec >= HELPED)(out.wait_sends)
    pl.when(sec >= HELPERS)(help_out.wait_sends)
    pl.when(sec < HELPED)(helped_out.wait_sends)

    for slot in range(PATCHES):
        pltpu.make_async_copy(fresh.at[slot], kv_h.at[slot], store_sem.at[0, slot]).wait()
        pltpu.make_async_copy(out_rows.at[slot], out_h.at[slot], store_sem.at[1, slot]).wait()

    for slot in range(PATCHES):
        @pl.when(sec == 0 if slot < PATCHES - 1 else is_even)
        def _():
            for chunk in range(CHUNKS):
                near_copy(slot, chunk).wait_send()

        @pl.when(sec < NSEC - 1 if slot < PATCHES - 1 else is_even)
        def _():
            for chunk in range(CHUNKS):
                next_copy(slot, chunk, True).wait_send()

    @pl.when(sec < NSEC - 1)
    def _():
        for slot in range(PATCHES):
            for chunk in range(CHUNKS):
                next_copy(slot, chunk, False).wait_send()


def to_patch_order(order_s, rows_in, kv_in, rows_out, kv_out):
    rows_out[...] = rows_in[...]
    kv_out[...] = kv_in[...]


def on_device(hidden, stale_kv, w_qkv, w_out, q_gain, k_gain, mod_table, pattern, step_index, order):
    vmem, smem, anywhere = (
        pl.BlockSpec(memory_space=pltpu.VMEM),
        pl.BlockSpec(memory_space=pltpu.SMEM),
        pl.BlockSpec(memory_space=pl.ANY),
    )
    bf16, f32 = jnp.bfloat16, jnp.float32
    dma = pltpu.SemaphoreType.DMA
    rows_slots, kv_slots = pl.pallas_call(
        kernel,
        out_shape=(
            jax.ShapeDtypeStruct((PATCHES, ROWS, D), bf16),
            jax.ShapeDtypeStruct((PATCHES, ROWS, 2 * INNER), bf16),
        ),
        in_specs=[smem] * 3 + [anywhere] * 4 + [vmem] * 3,
        out_specs=(anywhere, anywhere),
        scratch_shapes=[
            pltpu.VMEM((D, 3 * INNER), bf16),
            pltpu.VMEM((INNER, D), bf16),
            pltpu.VMEM((INNER, D), bf16),
            pltpu.VMEM((2 * SEQ_DEV, INNER), bf16),
            pltpu.VMEM((2 * SEQ_DEV, INNER), bf16),
            pltpu.VMEM((PATCHES, ROWS, D), bf16),
            pltpu.VMEM((PATCHES, ROWS, D), bf16),
            pltpu.VMEM((4 * PATCHES, D), f32),
            pltpu.VMEM((4 * PATCHES, D), f32),
            pltpu.VMEM((PATCHES, ROWS, 2 * INNER), bf16),
            pltpu.VMEM((PATCHES, ROWS, D), bf16),
            pltpu.VMEM((PATCHES, ROWS, 2 * INNER), bf16),
            pltpu.VMEM((PATCHES, ROWS, D), bf16),
            pltpu.VMEM((2 * ROWS, D), bf16),
            pltpu.VMEM((ROWS, INNER), bf16),
            pltpu.VMEM((ROWS, INNER), bf16),
            pltpu.VMEM((2 * (PATCHES - 1), ROWS, INNER), bf16),
            dma((NBLK,)),
            dma((NBLK,)),
            dma((NBLK,)),
            dma((NBLK,)),
            dma((31,)),
            dma((31,)),
            dma((31,)),
            dma((62,)),
            dma((1,)),
            dma((4,)),
            dma((PATCHES, CHUNKS)),
            dma((PATCHES, CHUNKS)),
            dma((PATCHES, CHUNKS)),
            dma((PATCHES, CHUNKS)),
            dma((PATCHES, CHUNKS)),
            pltpu.SemaphoreType.REGULAR,
            dma((2, PATCHES)),
            dma((2 * (PATCHES - 1),)),
            dma((2 * (PATCHES - 1),)),
            dma((2 * (PATCHES - 1),)),
            dma((2 * (PATCHES - 1),)),
            dma(()),
            dma(()),
        ],
        compiler_params=pltpu.CompilerParams(
            collective_id=0, has_side_effects=True, vmem_limit_bytes=63 * 1024 * 1024
        ),
        name="pipeline",
    )(
        order, step_index, pattern,
        hidden.reshape(PATCHES, ROWS, D), stale_kv.reshape(PATCHES, ROWS, 2 * INNER), w_qkv[0], w_out[0],
        q_gain, k_gain, mod_table.reshape(TSTEPS * 3, D),
    )

    def slot_of(patch, order_ref):
        slot = jnp.int32(0)
        for index in range(1, PATCHES):
            slot = jnp.where(order_ref[index] == patch, index, slot)
        return (slot, 0, 0)

    layer_out, kv_cache = pl.pallas_call(
        to_patch_order,
        out_shape=(
            jax.ShapeDtypeStruct((PATCHES, ROWS, D), bf16),
            jax.ShapeDtypeStruct((PATCHES, ROWS, 2 * INNER), bf16),
        ),
        grid_spec=pltpu.PrefetchScalarGridSpec(
            num_scalar_prefetch=1,
            grid=(PATCHES,),
            in_specs=[pl.BlockSpec((1, ROWS, D), slot_of), pl.BlockSpec((1, ROWS, 2 * INNER), slot_of)],
            out_specs=[
                pl.BlockSpec((1, ROWS, D), lambda patch, order_ref: (patch, 0, 0)),
                pl.BlockSpec((1, ROWS, 2 * INNER), lambda patch, order_ref: (patch, 0, 0)),
            ],
        ),
        name="patch_order",
    )(order, rows_slots, kv_slots)
    return (layer_out.reshape(1, SEQ_DEV, D), kv_cache.reshape(1, SEQ_DEV, 2 * INNER))


def solution(mesh):
    in_specs = (
        P("blk", None),
        P("section", "blk", None),
        P("section", "blk", None),
        P("section", "blk", None),
        P("section", None),
        P("section", None),
        P("section", None, None, None),
        P("blk", None),
        P("blk"),
        P(),
    )
    out_specs = (P("section", "blk", None), P("section", "blk", None))
    return jax.shard_map(
        on_device, mesh=mesh, in_specs=in_specs, out_specs=out_specs, check_vma=False
    )
```

```python
import functools
import math

import jax
import jax.numpy as jnp
from jax import lax
from jax.experimental import pallas as pl
from jax.experimental.pallas import tpu as pltpu
from jax.sharding import PartitionSpec as P

MESH = pl.DeviceIdType.MESH

D = 1536
HEADS = 12
HDIM = 128
PATCHES = 4
TSTEPS = 16
ROWS = 128
SEQ_DEV = PATCHES * ROWS
INNER = HEADS * HDIM
NY, NZ = 4, 8
NBLK = NY * NZ
NSEC = 8
SHARD = D // NBLK
NORM_EPS = 1e-06
CHUNK = 768
CHUNKS = INNER // CHUNK
SPLIT = 2560
OFFSETS = (0, 1, -1, 2, -2, 3, 4, 5)
FAR_UP, FAR_DOWN = 5, 2
PARTWAY = 2
LAG = 1
HELPED = 2
HELPERS = NSEC - HELPED
SCORE_SCALE = math.log2(math.e) / math.sqrt(HDIM)


def head_norm(values, gain_row):
    square = jnp.mean(values * values, axis=-1, keepdims=True)
    return values * lax.rsqrt(square + NORM_EPS) * gain_row


def modulate(rows, scale, shift):
    values = rows.astype(jnp.float32)
    centre = values - jnp.mean(values, axis=-1, keepdims=True)
    spread = jnp.mean(centre * centre, axis=-1, keepdims=True)
    return (centre * lax.rsqrt(spread + NORM_EPS) * (1.0 + scale) + shift).astype(jnp.bfloat16)


def kernel(
    order_s, step_s, pattern_s, hidden_h, stale_h, wq_h, wo_h, qgain, kgain, mod_table,
    out_h, kv_h,
    wq, wo, wo_help, keys, values, x_own, x_near, mod_own, mod_near, stale, hidden, fresh, out_rows, modulated, queries, attended, relay,
    recv_a, recv_b, recv_o, recv_h, send_a, send_b, send_o, send_h, send_x, local, rx_own, rx_near, tx_own, tx_near, tx_next, go, store_sem, rx_stale, tx_stale, rx_relay, tx_relay, rx_mod, tx_mod,
):
    sec = lax.axis_index("section")
    blk = lax.axis_index("blk")
    y, z = blk // NZ, lax.rem(blk, NZ)

    def at(yy, zz):
        return lax.rem(yy + 2 * NY, NY) * NZ + lax.rem(zz + 2 * NZ, NZ)

    up, down = lax.rem(sec + 1, NSEC), lax.rem(sec + NSEC - 1, NSEC)
    after, before = lax.rem(blk + 1, NBLK), lax.rem(blk + NBLK - 1, NBLK)
    chip_up, chip_down = lax.rem(sec + 2, NSEC), lax.rem(sec + NSEC - 2, NSEC)
    zp, zm, yp, ym = at(y, z + 1), at(y, z - 1), at(y + 1, z), at(y - 1, z)

    load_hidden = pltpu.make_async_copy(hidden_h, hidden, local.at[0])
    load_stale = pltpu.make_async_copy(stale_h, stale, local.at[1])
    load_wq = pltpu.make_async_copy(wq_h, wq.at[pl.ds(blk * SHARD, SHARD)], local.at[2])
    load_wo = pltpu.make_async_copy(wo_h, wo.at[pl.ds(blk * SHARD, SHARD)], local.at[3])
    load_stale.start()
    load_hidden.start()
    load_wq.start()
    load_wo.start()

    barrier = pltpu.get_barrier_semaphore()
    for target in (
        (sec, zp), (sec, zm), (sec, yp), (sec, ym), (sec, after), (sec, before),
        (up, blk), (down, blk), (up, after), (down, before), (chip_up, blk), (chip_down, blk),
    ):
        pl.semaphore_signal(barrier, inc=1, device_id=target, device_id_type=MESH)
    pl.semaphore_wait(barrier, 12)


    class Gather:
        def __init__(self, buffer, start, stop, recv, send, source):
            self.buffer, self.columns = buffer, pl.ds(start, stop - start)
            self.recv, self.send, self.source = recv, send, source
            self.count = 0

        def rows(self, shard):
            return self.buffer.at[pl.ds(pl.multiple_of(shard * SHARD, 16), SHARD), self.columns]

        def push(self, shard, *targets, from_input=False, to=None):
            for target in targets:
                copy = pltpu.make_async_remote_copy(
                    src_ref=self.source.at[:, self.columns] if from_input else self.rows(shard),
                    dst_ref=(self if to is None else to).rows(shard),
                    send_sem=self.send.at[self.count],
                    recv_sem=(self if to is None else to).recv.at[shard],
                    device_id=target if isinstance(target, tuple) else (sec, target),
                    device_id_type=MESH,
                )
                copy.start()
                self.count += 1

        def arrived(self, shard):
            pltpu.make_async_remote_copy(
                src_ref=self.rows(shard), dst_ref=self.rows(shard), send_sem=self.send.at[0],
                recv_sem=self.recv.at[shard], device_id=(up, blk), device_id_type=MESH,
            ).wait_recv()

        def along(self, shard, k):
            if OFFSETS[k] == 0:
                self.push(shard, zp, zm)
            elif 0 < OFFSETS[k] < FAR_UP:
                self.push(shard, zm)
            elif -FAR_DOWN < OFFSETS[k] < 0:
                self.push(shard, zp)

        def cross(self, k, level):
            zk = z + OFFSETS[k]
            here, there = at(y - 1, zk), at(y + 1, zk)
            self.arrived(here)
            self.arrived(there)
            if level:
                odd = lax.rem(zk + 2 * NZ, 2) == 1
                self.push(jnp.where(odd, there, here), jnp.where(odd, ym, yp))
            else:
                self.push(there, ym)
            return here, there

        def ring_step(self, k):
            shard = at(y, z + OFFSETS[k])
            self.arrived(shard)
            self.along(shard, k)
            self.push(shard, yp, ym)
            if k > 0:
                self.cross(k - 1, True)

        def wait_sends(self):
            for index in range(self.count):
                pltpu.make_async_remote_copy(
                    src_ref=self.rows(blk), dst_ref=self.rows(blk), send_sem=self.send.at[index],
                    recv_sem=self.recv.at[blk], device_id=(up, blk), device_id_type=MESH,
                ).wait_send()

    main = Gather(wq, 0, SPLIT, recv_a, send_a, wq_h)
    side = Gather(wq, SPLIT, 3 * INNER, recv_b, send_b, wq_h)
    out = Gather(wo, 0, D, recv_o, send_o, wo_h)
    help_out = Gather(wo_help, 0, D, recv_h, send_h, wo_h)
    helped_out = Gather(wo, 0, D, recv_o, send_x, wo_h)

    @pl.when(sec < HELPED)
    def _():
        helped_out.push(blk, (chip_down, blk), from_input=True, to=help_out)

    is_even = lax.rem(sec, 2) == 0

    def let_go():
        pl.semaphore_signal(go, inc=1, device_id=(up, blk), device_id_type=MESH)

    @pl.when(jnp.logical_not(is_even))
    def _():
        pl.semaphore_wait(go, 1)

    @pl.when(sec >= HELPERS)
    def _():
        for k in range(NZ):
            shard = at(y, z + OFFSETS[k])
            help_out.arrived(shard)
            help_out.along(shard, k)
            help_out.push(shard, yp, ym)
            if k > 0:
                help_out.push(shard, (chip_up, blk), to=helped_out)
                for shard in help_out.cross(k - 1, True):
                    help_out.push(shard, (chip_up, blk), to=helped_out)
            if k > 1:
                shard = at(y + 2, z + OFFSETS[k - 2])
                help_out.arrived(shard)
                help_out.push(shard, (chip_up, blk), to=helped_out)
        for shard in help_out.cross(NZ - 1, True):
            help_out.push(shard, (chip_up, blk), to=helped_out)
        for k in (NZ - 2, NZ - 1):
            shard = at(y + 2, z + OFFSETS[k])
            help_out.arrived(shard)
            help_out.push(shard, (chip_up, blk), to=helped_out)

    pl.when(sec == HELPERS)(let_go)
    side.push(blk, yp, ym, from_input=True)
    main.push(blk, zp, zm, yp, ym, from_input=True)
    side.push(blk, zp, zm, from_input=True)

    @pl.when(sec >= HELPED)
    def _():
        out.push(blk, zp, zm, yp, ym, from_input=True)

    for slot in range(PATCHES):
        step = step_s[order_s[slot]]
        for row in range(3):
            mod_own[pl.ds(4 * slot + row, 1), :] = mod_table[pl.ds(3 * step + row, 1), :]
    send_mod = pltpu.make_async_remote_copy(
        src_ref=mod_own, dst_ref=mod_near, send_sem=tx_mod, recv_sem=rx_mod,
        device_id=(sec, after), device_id_type=MESH,
    )
    send_mod.start()

    load_hidden.wait()

    def near_copy(slot, chunk):
        columns = pl.ds(chunk * CHUNK, CHUNK)
        return pltpu.make_async_remote_copy(
            src_ref=x_own.at[slot, :, columns], dst_ref=x_near.at[slot, :, columns],
            send_sem=tx_near.at[slot, chunk], recv_sem=rx_near.at[slot, chunk],
            device_id=(sec, after), device_id_type=MESH,
        )

    def next_copy(slot, chunk, near):
        columns = pl.ds(pl.multiple_of(chunk * CHUNK, CHUNK), CHUNK)
        landing, tx, rx, target = (x_near, tx_next, rx_near, after) if near else (x_own, tx_own, rx_own, blk)
        return pltpu.make_async_remote_copy(
            src_ref=out_rows.at[slot, :, columns], dst_ref=landing.at[slot, :, columns],
            send_sem=tx.at[slot, chunk], recv_sem=rx.at[slot, chunk],
            device_id=(up, target), device_id_type=MESH,
        )

    @pl.when(sec == 0)
    def _():
        for slot in range(PATCHES):
            x_own[slot] = hidden[order_s[slot]]
        for chunk in range(CHUNKS):
            near_copy(0, chunk).start()

    load_stale.wait()
    for slot in range(1, PATCHES):
        patch = order_s[slot]
        for head in range(HEADS):
            columns = pl.ds(head * HDIM, HDIM)
            keys[pl.ds(slot * ROWS, ROWS), columns] = head_norm(
                stale[patch, :, columns].astype(jnp.float32), kgain[...]
            ).astype(jnp.bfloat16)
        values[pl.ds(slot * ROWS, ROWS), :] = stale[patch, :, INNER:]
    pieces = 2 * (PATCHES - 1)
    by_relay = jnp.logical_and(jnp.logical_not(is_even), z == NZ - 1)

    def stale_rows(i, half):
        buffer = (keys, values)[i % 2]
        return buffer.at[pl.ds(half * SEQ_DEV + (i // 2 + 1) * ROWS, ROWS)]

    def stale_copy(i):
        return pltpu.make_async_remote_copy(
            src_ref=stale_rows(i, 0), dst_ref=stale_rows(i, 1), send_sem=tx_stale.at[i], recv_sem=rx_stale.at[i],
            device_id=(sec, after), device_id_type=MESH,
        )

    def relay_copy(i, second):
        return pltpu.make_async_remote_copy(
            src_ref=relay.at[i] if second else stale_rows(i, 0),
            dst_ref=stale_rows(i, 1) if second else relay.at[i],
            send_sem=(tx_relay if second else tx_stale).at[i],
            recv_sem=(rx_stale if second else rx_relay).at[i],
            device_id=(sec, zp if second else yp), device_id_type=MESH,
        )

    def between(k):
        if 1 <= k <= pieces:
            @pl.when(by_relay)
            def _():
                relay_copy(k - 1, False).start()

            @pl.when(jnp.logical_not(by_relay))
            def _():
                stale_copy(k - 1).start()

        if 3 <= k < pieces + 3:
            @pl.when(by_relay)
            def _():
                relay_copy(k - 3, False).wait_recv()
                relay_copy(k - 3, True).start()

        if k == PARTWAY:
            pl.when(jnp.logical_and(is_even, sec < HELPERS))(let_go)

    side.arrived(ym)
    side.arrived(yp)
    side.push(yp, ym)
    side.push(ym, zp, zm)
    side.push(yp, zp, zm)
    for k in range(1, NZ):
        shard = at(y, z + OFFSETS[k])
        main.arrived(shard)
        main.along(shard, k)
        main.push(shard, yp, ym)
        if k == 1:
            side.arrived(at(y + 2, z))
            side.push(at(y + 2, z), zp, zm)
        main.cross(k - 1, False)
        for i in range(NY):
            shard = at(y + i, z + OFFSETS[k])
            side.arrived(shard)
            side.along(shard, k)
        between(k)
        if k > LAG:
            pl.when(sec >= HELPED)(functools.partial(out.ring_step, k - LAG))
    main.cross(NZ - 1, False)
    for k in range(NZ):
        main.arrived(at(y + 2, z + OFFSETS[k]))
    between(NZ)

    @pl.when(sec == 0)
    def _():
        for chunk in range(CHUNKS):
            near_copy(1, chunk).start()

    @pl.when(sec >= HELPED)
    def _():
        for k in range(NZ - LAG, NZ):
            out.ring_step(k)
        out.cross(NZ - 1, True)
        for k in range(NZ):
            out.arrived(at(y + 2, z + OFFSETS[k]))

    load_wq.wait()
    load_wo.wait()
    send_mod.wait()
    for i in range(pieces):
        stale_copy(i).wait()

    @pl.when(by_relay)
    def _():
        for i in range(pieces):
            relay_copy(i, True).wait_send()

    def slot_step(slot, carry):
        @pl.when(jnp.logical_and(sec == 0, slot < PATCHES - 2))
        def _():
            for chunk in range(CHUNKS):
                near_copy(slot + 2, chunk).start()

        @pl.when(sec > 0)
        def _():
            for chunk in range(CHUNKS):
                next_copy(slot, chunk, False).wait_recv()

                @pl.when(jnp.logical_and(is_even, slot == PATCHES - 1))
                def _():
                    near_copy(slot, chunk).start()

        modulated[pl.ds(0, ROWS), :] = modulate(
            x_own[slot], mod_own[pl.ds(4 * slot + 1, 1), :], mod_own[pl.ds(4 * slot, 1), :]
        )
        own_rows = pl.ds(pl.multiple_of(slot * ROWS, ROWS), ROWS)
        near_rows = pl.ds(pl.multiple_of(SEQ_DEV + slot * ROWS, ROWS), ROWS)

        def project_q(chunk, carry):
            base = pl.multiple_of(chunk * CHUNK, CHUNK)
            product = jnp.dot(
                modulated[pl.ds(0, ROWS), :], wq[:, pl.ds(base, CHUNK)], preferred_element_type=jnp.float32
            )
            for head in range(CHUNK // HDIM):
                queries[:, pl.ds(base + head * HDIM, HDIM)] = head_norm(
                    product[:, head * HDIM:(head + 1) * HDIM], qgain[...]
                ).astype(jnp.bfloat16)
            return carry

        def project_k(chunk, carry):
            base = pl.multiple_of(chunk * CHUNK, CHUNK)
            product = jnp.dot(
                modulated[...], wq[:, pl.ds(INNER + base, CHUNK)], preferred_element_type=jnp.float32
            ).astype(jnp.bfloat16)
            fresh[slot, :, pl.ds(base, CHUNK)] = product[:ROWS]
            for head in range(CHUNK // HDIM):
                normed = head_norm(
                    product[:, head * HDIM:(head + 1) * HDIM].astype(jnp.float32), kgain[...]
                ).astype(jnp.bfloat16)
                columns = pl.ds(base + head * HDIM, HDIM)
                keys[own_rows, columns] = normed[:ROWS]
                keys[near_rows, columns] = normed[ROWS:]
            return carry

        def project_v(chunk, carry):
            base = pl.multiple_of(chunk * CHUNK, CHUNK)
            product = jnp.dot(
                modulated[...], wq[:, pl.ds(2 * INNER + base, CHUNK)], preferred_element_type=jnp.float32
            ).astype(jnp.bfloat16)
            fresh[slot, :, pl.ds(INNER + base, CHUNK)] = product[:ROWS]
            values[own_rows, pl.ds(base, CHUNK)] = product[:ROWS]
            values[near_rows, pl.ds(base, CHUNK)] = product[ROWS:]
            return carry

        lax.fori_loop(0, CHUNKS, project_q, 0)
        for chunk in range(CHUNKS):
            near_copy(slot, chunk).wait_recv()
        modulated[pl.ds(ROWS, ROWS), :] = modulate(
            x_near[slot], mod_near[pl.ds(4 * slot + 1, 1), :], mod_near[pl.ds(4 * slot, 1), :]
        )
        lax.fori_loop(0, CHUNKS, project_k, 0)
        lax.fori_loop(0, CHUNKS, project_v, 0)
        pltpu.make_async_copy(fresh.at[slot], kv_h.at[slot], store_sem.at[0, slot]).start()

        patch = order_s[slot]
        masks = [
            pattern_s[patch, half * PATCHES + order_s[j]].astype(jnp.float32) for half in range(2) for j in range(PATCHES)
        ]

        def attend(head, carry):
            columns = pl.ds(pl.multiple_of(head * HDIM, HDIM), HDIM)
            scores = lax.dot_general(
                queries[:, columns], keys[:, columns], (((1,), (1,)), ((), ())), preferred_element_type=jnp.float32
            )
            tiles = [
                jnp.exp2(scores[:, j * ROWS:(j + 1) * ROWS] * SCORE_SCALE) * masks[j] for j in range(2 * PATCHES)
            ]
            total = tiles[0]
            for tile in tiles[1:]:
                total = total + tile
            weight_sum = jnp.sum(total, axis=-1, keepdims=True)
            probs = jnp.concatenate([tile.astype(jnp.bfloat16) for tile in tiles], axis=1)
            mixture = jnp.dot(probs, values[:, columns], preferred_element_type=jnp.float32)
            attended[:, columns] = (mixture / weight_sum).astype(jnp.bfloat16)
            return carry

        lax.fori_loop(0, HEADS, attend, 0, unroll=6)

        def project_out(chunk, carry):
            columns = pl.ds(pl.multiple_of(chunk * CHUNK, CHUNK), CHUNK)
            product = jnp.dot(attended[...], wo[:, columns], preferred_element_type=jnp.float32)
            out_rows[slot, :, columns] = (
                x_own[slot, :, columns].astype(jnp.float32) + mod_own[pl.ds(4 * slot + 2, 1), columns] * product
            ).astype(jnp.bfloat16)

            @pl.when(sec < NSEC - 1)
            def _():
                next_copy(slot, chunk, False).start()

                @pl.when(is_even)
                def _():
                    next_copy(slot, chunk, True).start()

            return carry

        @pl.when(jnp.logical_and(sec < HELPED, slot == 0))
        def _():
            for i in range(NBLK - 1):
                helped_out.arrived(lax.rem(blk + 1 + i, NBLK))

        lax.fori_loop(0, CHUNKS, project_out, 0)

        @pl.when(jnp.logical_and(jnp.logical_not(is_even), jnp.logical_and(sec < NSEC - 1, slot < PATCHES - 1)))
        def _():
            for chunk in range(CHUNKS):
                next_copy(slot, chunk, True).start()

        pltpu.make_async_copy(out_rows.at[slot], out_h.at[slot], store_sem.at[1, slot]).start()
        return carry

    lax.fori_loop(0, PATCHES, slot_step, 0)

    main.wait_sends()
    side.wait_sends()

    pl.when(sec >= HELPED)(out.wait_sends)
    pl.when(sec >= HELPERS)(help_out.wait_sends)
    pl.when(sec < HELPED)(helped_out.wait_sends)

    for slot in range(PATCHES):
        pltpu.make_async_copy(fresh.at[slot], kv_h.at[slot], store_sem.at[0, slot]).wait()
        pltpu.make_async_copy(out_rows.at[slot], out_h.at[slot], store_sem.at[1, slot]).wait()

    for slot in range(PATCHES):
        @pl.when(sec == 0 if slot < PATCHES - 1 else is_even)
        def _():
            for chunk in range(CHUNKS):
                near_copy(slot, chunk).wait_send()

        @pl.when(sec < NSEC - 1 if slot < PATCHES - 1 else is_even)
        def _():
            for chunk in range(CHUNKS):
                next_copy(slot, chunk, True).wait_send()

    @pl.when(sec < NSEC - 1)
    def _():
        for slot in range(PATCHES):
            for chunk in range(CHUNKS):
                next_copy(slot, chunk, False).wait_send()


def to_patch_order(order_s, rows_in, kv_in, rows_out, kv_out):
    rows_out[...] = rows_in[...]
    kv_out[...] = kv_in[...]


def on_device(hidden, stale_kv, w_qkv, w_out, q_gain, k_gain, mod_table, pattern, step_index, order):
    vmem, smem, anywhere = (
        pl.BlockSpec(memory_space=pltpu.VMEM),
        pl.BlockSpec(memory_space=pltpu.SMEM),
        pl.BlockSpec(memory_space=pl.ANY),
    )
    bf16, f32 = jnp.bfloat16, jnp.float32
    dma = pltpu.SemaphoreType.DMA
    rows_slots, kv_slots = pl.pallas_call(
        kernel,
        out_shape=(
            jax.ShapeDtypeStruct((PATCHES, ROWS, D), bf16),
            jax.ShapeDtypeStruct((PATCHES, ROWS, 2 * INNER), bf16),
        ),
        in_specs=[smem] * 3 + [anywhere] * 4 + [vmem] * 3,
        out_specs=(anywhere, anywhere),
        scratch_shapes=[
            pltpu.VMEM((D, 3 * INNER), bf16),
            pltpu.VMEM((INNER, D), bf16),
            pltpu.VMEM((INNER, D), bf16),
            pltpu.VMEM((2 * SEQ_DEV, INNER), bf16),
            pltpu.VMEM((2 * SEQ_DEV, INNER), bf16),
            pltpu.VMEM((PATCHES, ROWS, D), bf16),
            pltpu.VMEM((PATCHES, ROWS, D), bf16),
            pltpu.VMEM((4 * PATCHES, D), f32),
            pltpu.VMEM((4 * PATCHES, D), f32),
            pltpu.VMEM((PATCHES, ROWS, 2 * INNER), bf16),
            pltpu.VMEM((PATCHES, ROWS, D), bf16),
            pltpu.VMEM((PATCHES, ROWS, 2 * INNER), bf16),
            pltpu.VMEM((PATCHES, ROWS, D), bf16),
            pltpu.VMEM((2 * ROWS, D), bf16),
            pltpu.VMEM((ROWS, INNER), bf16),
            pltpu.VMEM((ROWS, INNER), bf16),
            pltpu.VMEM((2 * (PATCHES - 1), ROWS, INNER), bf16),
            dma((NBLK,)),
            dma((NBLK,)),
            dma((NBLK,)),
            dma((NBLK,)),
            dma((31,)),
            dma((31,)),
            dma((31,)),
            dma((62,)),
            dma((1,)),
            dma((4,)),
            dma((PATCHES, CHUNKS)),
            dma((PATCHES, CHUNKS)),
            dma((PATCHES, CHUNKS)),
            dma((PATCHES, CHUNKS)),
            dma((PATCHES, CHUNKS)),
            pltpu.SemaphoreType.REGULAR,
            dma((2, PATCHES)),
            dma((2 * (PATCHES - 1),)),
            dma((2 * (PATCHES - 1),)),
            dma((2 * (PATCHES - 1),)),
            dma((2 * (PATCHES - 1),)),
            dma(()),
            dma(()),
        ],
        compiler_params=pltpu.CompilerParams(
            collective_id=0, has_side_effects=True, vmem_limit_bytes=63 * 1024 * 1024
        ),
        name="pipeline",
    )(
        order, step_index, pattern,
        hidden.reshape(PATCHES, ROWS, D), stale_kv.reshape(PATCHES, ROWS, 2 * INNER), w_qkv[0], w_out[0],
        q_gain, k_gain, mod_table.reshape(TSTEPS * 3, D),
    )

    def slot_of(patch, order_ref):
        slot = jnp.int32(0)
        for index in range(1, PATCHES):
            slot = jnp.where(order_ref[index] == patch, index, slot)
        return (slot, 0, 0)

    layer_out, kv_cache = pl.pallas_call(
        to_patch_order,
        out_shape=(
            jax.ShapeDtypeStruct((PATCHES, ROWS, D), bf16),
            jax.ShapeDtypeStruct((PATCHES, ROWS, 2 * INNER), bf16),
        ),
        grid_spec=pltpu.PrefetchScalarGridSpec(
            num_scalar_prefetch=1,
            grid=(PATCHES,),
            in_specs=[pl.BlockSpec((1, ROWS, D), slot_of), pl.BlockSpec((1, ROWS, 2 * INNER), slot_of)],
            out_specs=[
                pl.BlockSpec((1, ROWS, D), lambda patch, order_ref: (patch, 0, 0)),
                pl.BlockSpec((1, ROWS, 2 * INNER), lambda patch, order_ref: (patch, 0, 0)),
            ],
        ),
        name="patch_order",
    )(order, rows_slots, kv_slots)
    return (layer_out.reshape(1, SEQ_DEV, D), kv_cache.reshape(1, SEQ_DEV, 2 * INNER))


def solution(mesh):
    in_specs = (
        P("blk", None),
        P("section", "blk", None),
        P("section", "blk", None),
        P("section", "blk", None),
        P("section", None),
        P("section", None),
        P("section", None, None, None),
        P("blk", None),
        P("blk"),
        P(),
    )
    out_specs = (P("section", "blk", None), P("section", "blk", None))
    return jax.shard_map(
        on_device, mesh=mesh, in_specs=in_specs, out_specs=out_specs, check_vma=False
    )
```
